32 devices in a mesh: occ: 16 (over z, y, x), grp: 2 (over core).
Axes of the slice: x: 2, y: 2, z: 4, core: 2. Of those that a mesh axis runs over, the one named last changes fastest.
Arguments:
- b_factors: bfloat16 [32, 512, 768], P(('occ', 'grp')), may hold values from -0.29882812 to 0.29882812
- occ_energy: float32 [32], replicated, may hold values from -2 to -0.5
- vir_energy: float32 [512], replicated, may hold values from 0.2 to 3
- integrals: bfloat16 [512, 768, 1024], P('grp', 'occ'), may hold values from -0.0625 to 0.0625
- window_start: int32 [1], replicated, may hold values from 0 to 15
Outputs:
- aux_metric: float32 [768, 768], P('occ', 'grp')
- lagrangian: float32 [32, 1024], P('occ', 'grp')
The draws below stay inside these ranges and needn't reach their ends.
Inputs may be any that keep to these rules, and one draw needn't show every extreme that they name: `window_start`: the cycle offset of the window's first pair.
All inputs are finite; a program needn't handle non-finite values.
Results may differ from the reference program's by a relative error of at most 0.0034.
Values may be sent and summed in bfloat16 or wider, within the bound.
A program may use at most 128 MiB of HBM per device.

```python
import math
import jax
import jax.numpy as jnp
from jax import lax

V = 512
NAUX = 768
NORB = 1024
SHIFTS = 3
O = 32
N_OCC = 16
N_GRP = 2


def steps_of(stream_key, dims, pieces, smallest, top_value):
    def one(position, shards_of):
        steps = jax.random.uniform(jax.random.fold_in(jax.random.fold_in(stream_key, 6), position), (shards_of,), jnp.float32, smallest / len(pieces), top_value / len(pieces))
        return jnp.repeat(jnp.exp(steps), dims[position] // shards_of).reshape((-1,) + (1,) * (len(dims) - position - 1))

    gain = one(*pieces[0])
    for cut in pieces[1:]:
        gain = gain * one(*cut)
    return gain


def noise(rng, shape, spread, reach, cuts=(), held_as=jnp.bfloat16):
    values = spread * jax.random.normal(rng, shape, jnp.float32)
    if cuts:
        values = values * steps_of(rng, shape, cuts, -0.22, 0.18)
    return jnp.clip(values, -reach, reach).astype(held_as)


def setup_inputs(seed: int = 0) -> dict:
    arg_keys = jax.random.split(jax.random.key(seed), 6)
    b_factors = noise(arg_keys[0], (O, V, NAUX), 0.05, 0.29882812, ((0, 32),))
    occ_energy = jnp.clip(jax.random.uniform(arg_keys[1], (O,), jnp.float32, -2.0, -0.5), -2.0, -0.5)
    vir_energy = jnp.clip(jnp.exp(jax.random.uniform(arg_keys[2], (V,), jnp.float32, math.log(0.2), math.log(3.0))), 0.2, 3.0)
    integrals = noise(arg_keys[3], (V, NAUX, NORB), (V * NAUX // 50) ** -0.5, 0.0625, ((0, 2), (1, 16)))
    window_start = jax.random.randint(arg_keys[4], (1,), 0, N_OCC).astype(jnp.int32)
    return {"b_factors": b_factors, "occ_energy": occ_energy, "vir_energy": vir_energy, "integrals": integrals, "window_start": window_start}


def reference(b_factors, occ_energy, vir_energy, integrals, window_start):
    offset = window_start[0]

    def per_orbital(orbital):
        cycle_pos = orbital // N_GRP
        group_pos = orbital % N_GRP
        own_rows = b_factors[orbital]
        total = jnp.zeros((V, NAUX), jnp.float32)
        for step_no in range(SHIFTS):
            partner = (jnp.mod(cycle_pos - offset - step_no, N_OCC) * N_GRP + group_pos).astype(jnp.int32)
            other_rows = lax.dynamic_index_in_dim(b_factors, partner, 0, keepdims=False)
            intersection = lax.dot_general(own_rows, other_rows, (((1,), (1,)), ((), ())), preferred_element_type=jnp.float32)
            denominator = occ_energy[orbital] + occ_energy[partner] - vir_energy[:, None] - vir_energy[None, :]
            amplitude = intersection / denominator
            combined = (2.0 * amplitude - amplitude.T).astype(jnp.bfloat16)
            total = total + jnp.dot(combined, other_rows, preferred_element_type=jnp.float32)
        return total.astype(jnp.bfloat16)

    density = lax.map(per_orbital, jnp.arange(O, dtype=jnp.int32))
    flat_density = density.reshape(O * V, NAUX)
    aux_metric = jnp.dot(flat_density.T, b_factors.reshape(O * V, NAUX), preferred_element_type=jnp.float32)
    lagrangian = jnp.dot(density.reshape(O, V * NAUX), integrals.reshape(V * NAUX, NORB), preferred_element_type=jnp.float32)
    return aux_metric, lagrangian
```

```python
import functools
import math

import jax
import jax.numpy as jnp
from jax import lax
from jax.experimental import pallas as pl
from jax.experimental.pallas import tpu as pltpu
from jax.sharding import PartitionSpec as P

MESH = pl.DeviceIdType.MESH


def work_of(cyc, grp, n_cycle, n_group):
    return cyc - cyc % 2 + grp % 2, grp - grp % 2 + cyc % 2


def spread(x, by):
    n_cycle, n_group = lax.axis_size("occ"), lax.axis_size("grp")
    pairs = []
    for cyc in range(n_cycle):
        for grp in range(n_group):
            pos, group = work_of(cyc, grp, n_cycle, n_group)
            pairs.append((((pos + by) % n_cycle) * n_group + group, cyc * n_group + grp))
    return lax.ppermute(x, ("occ", "grp"), pairs)


def block_plan(n_vir, n_aux, n_cycle, n_group):
    aux_local, vir_local = n_aux // n_cycle, n_vir // n_group
    joined = 128 // math.gcd(aux_local, 128)
    lanes = joined * aux_local // 128
    halves = 2 if vir_local % (32 * joined) == 0 else 1
    return aux_local, vir_local, joined, lanes, halves, vir_local // joined // halves


def neighbour_kernel(
    n_cycle, n_group, chunks,
    own, here, near, far, hop, copy_sem, swap_ss, swap_rs, out_ss, hop_rs, fwd_ss, far_rs, near_ss, near_rs,
):
    cyc = lax.axis_index("occ")
    grp = lax.axis_index("grp")
    x, y, core = lax.rem(cyc, 2), lax.rem(cyc // 2, 2), lax.rem(grp, 2)
    size = own.shape[0] // chunks
    half = chunks // 2
    diagonal = (cyc + 1 - 2 * x, grp + 1 - 2 * core)
    twin = (cyc, grp + 1 - 2 * core)
    y_mate = (cyc + 2 - 4 * y, grp)
    above = (lax.rem(cyc + 4, n_cycle), grp)
    below = (lax.rem(cyc + n_cycle - 4, n_cycle), grp)
    barrier = pltpu.get_barrier_semaphore()
    for other in (twin, y_mate, below):
        pl.semaphore_signal(barrier, inc=1, device_id=other, device_id_type=MESH)

    @pl.when(x != core)
    def _():
        pl.semaphore_signal(barrier, inc=1, device_id=diagonal, device_id_type=MESH)

    pl.semaphore_wait(barrier, 3 + lax.rem(x + core, 2))

    def part(c):
        return pl.ds(c * size, size)

    def remote(src, dst, send_sem, recv_sem, to):
        return pltpu.make_async_remote_copy(
            src_ref=src, dst_ref=dst, send_sem=send_sem, recv_sem=recv_sem,
            device_id=to, device_id_type=MESH,
        )

    def swap_copy(c):
        return remote(own.at[part(c)], here.at[part(c)], swap_ss.at[c], swap_rs.at[c], diagonal)

    def near_copy(c, source):
        return remote(source.at[part(c)], near.at[part(c)], near_ss.at[c], near_rs.at[c], twin)

    def direct_copy(c, source):
        return remote(source.at[part(c)], far.at[part(c)], out_ss.at[c], far_rs.at[c], y_mate)

    def hop_copy(c, source):
        return remote(
            source.at[part(c)], hop.at[part(c % half)], out_ss.at[c], hop_rs.at[c % half],
            y_mate if c < half else above,
        )

    def up_copy(c):
        return remote(hop.at[part(c)], far.at[part(c)], fwd_ss.at[c], far_rs.at[c], above)

    def across_copy(c):
        return remote(
            hop.at[part(c)], far.at[part(c + half)], fwd_ss.at[c], far_rs.at[c + half], y_mate
        )

    def pass_on(c, source):
        @pl.when(y == 0)
        def _():
            direct_copy(c, source).start()

        @pl.when(y == 1)
        def _():
            hop_copy(c, source).start()

        @pl.when(core == 0)
        def _():
            near_copy(c, source).start()

    order = [c // 2 + half * (c % 2) for c in range(chunks)]
    keep = pltpu.make_async_copy(own, here, copy_sem)

    @pl.when(x == core)
    def _():
        for c in order:
            pass_on(c, own)
        keep.start()

    @pl.when(x != core)
    def _():
        for c in order:
            swap_copy(c).start()
        for c in order:
            swap_copy(c).wait_recv()
            pass_on(c, here)

    for c in range(half):
        hop_copy(c, own).wait_recv()

        @pl.when(y == 0)
        def _():
            up_copy(c).start()

        @pl.when(y == 1)
        def _():
            across_copy(c).start()

    for c in order:
        direct_copy(c, own).wait_recv()

        @pl.when(core == 1)
        def _():
            near_copy(c, far).start()

    for c in range(chunks):
        near_copy(c, far).wait_recv()
        near_copy(c, far).wait_send()
        direct_copy(c, own).wait_send()
    for c in range(half):
        up_copy(c).wait_send()

    @pl.when(x == core)
    def _():
        keep.wait()

    @pl.when(x != core)
    def _():
        for c in range(chunks):
            swap_copy(c).wait_send()


def neighbours(n_cycle, n_group, own_rows):
    n_vir, n_aux = own_rows.shape
    chunks = 8
    dma = pltpu.SemaphoreType.DMA
    anywhere = pl.BlockSpec(memory_space=pl.ANY)
    block = jax.ShapeDtypeStruct((n_vir, n_aux), own_rows.dtype)
    return pl.pallas_call(
        functools.partial(neighbour_kernel, n_cycle, n_group, chunks),
        out_shape=(block, block, block),
        in_specs=[anywhere],
        out_specs=(anywhere, anywhere, anywhere),
        scratch_shapes=[
            pltpu.VMEM((n_vir // 2, n_aux), own_rows.dtype), dma,
            dma((chunks,)), dma((chunks,)), dma((chunks,)), dma((chunks // 2,)),
            dma((chunks // 2,)), dma((chunks,)), dma((chunks,)), dma((chunks,)),
        ],
        compiler_params=pltpu.CompilerParams(
            collective_id=0, has_side_effects=True, vmem_limit_bytes=4 * 1024 * 1024
        ),
        cost_estimate=pl.CostEstimate(
            flops=0, bytes_accessed=60 * n_vir * n_aux, transcendentals=0
        ),
    )(own_rows)


def pair_kernel(
    n_cycle, n_group,
    own_ref, here_ref, near_ref, far_ref, energy_ref, start_ref, vir_row_ref, dens_out, blocks_out,
    total, stage, vir_col_ref,
):
    place, group = work_of(lax.axis_index("occ"), lax.axis_index("grp"), n_cycle, n_group)
    n_vir, n_aux = own_ref.shape
    vir_col_ref[...] = jnp.broadcast_to(vir_row_ref[...], (128, n_vir)).T
    shift = lax.rem(start_ref[0], n_cycle)
    own_energy = energy_ref[lax.rem(place + shift, n_cycle) * n_group + group]
    tall = min(256, n_vir)
    across = (((1,), (1,)), ((), ()))

    def term(other, step_no, put):
        partner = lax.rem(place - step_no + n_cycle, n_cycle)
        energy = own_energy + energy_ref[partner * n_group + group]

        @pl.loop(0, n_vir // tall)
        def _(k):
            at = pl.ds(pl.multiple_of(k * tall, tall), tall)
            straight = lax.dot_general(
                own_ref[at, :], other[...], across, preferred_element_type=jnp.float32
            )
            crossed = lax.dot_general(
                other[at, :], own_ref[...], across, preferred_element_type=jnp.float32
            )
            denominator = energy - vir_col_ref[at, 0:1] - vir_row_ref[...]
            combined = ((2.0 * straight - crossed) / denominator).astype(jnp.bfloat16)
            put(at, jnp.dot(combined, other[...], preferred_element_type=jnp.float32))

    def put_first(at, value):
        total[at, :] = value

    def put_next(at, value):
        total[at, :] += value

    def put_last(at, value):
        value = total[at, :] + value
        for b in range(n_aux // 128):
            stage[pl.ds(b * n_vir + at.start, tall), :] = value[:, b * 128:(b + 1) * 128]
        dens_out[at, :] = value.astype(dens_out.dtype)

    term(here_ref, 0, put_first)
    term(near_ref, 1, put_next)
    term(far_ref, 2, put_last)

    aux_local, vir_local, joined, lanes, halves, tall_block = block_plan(
        n_vir, n_aux, n_cycle, n_group
    )

    @pl.loop(0, n_group * halves)
    def _(k):
        g, h = k // halves, lax.rem(k, halves)
        first = k * (tall_block * joined)
        picked = [
            jnp.concatenate(
                [
                    stage[pl.ds(b * n_vir + first + j, tall_block, stride=joined), :]
                    for b in range(n_aux // 128)
                ],
                axis=1,
            )
            for j in range(joined)
        ]
        for o in range(n_cycle):
            wide = jnp.concatenate(
                [piece[:, o * aux_local:(o + 1) * aux_local] for piece in picked], axis=1
            ).astype(blocks_out.dtype)
            for c in range(lanes):
                blocks_out[o * n_group + g, h * lanes + c] = wide[:, c * 128:(c + 1) * 128]


def pair_densities(n_cycle, n_group, own_rows, here, near, far, occ_energy, vir_energy, window_start):
    n_vir, n_aux = own_rows.shape
    _, _, _, lanes, halves, tall_block = block_plan(n_vir, n_aux, n_cycle, n_group)
    smem = pl.BlockSpec(memory_space=pltpu.SMEM)
    vmem = pl.BlockSpec(memory_space=pltpu.VMEM)
    return pl.pallas_call(
        functools.partial(pair_kernel, n_cycle, n_group),
        out_shape=(
            jax.ShapeDtypeStruct((n_vir, n_aux), jnp.bfloat16),
            jax.ShapeDtypeStruct(
                (n_cycle * n_group, halves * lanes, tall_block, 128), jnp.bfloat16
            ),
        ),
        in_specs=[vmem, vmem, vmem, vmem, smem, smem, vmem],
        out_specs=(vmem, vmem),
        scratch_shapes=[
            pltpu.VMEM((n_vir, n_aux), jnp.float32),
            pltpu.VMEM((n_aux // 128 * n_vir, 128), jnp.float32),
            pltpu.VMEM((n_vir, 128), jnp.float32),
        ],
        compiler_params=pltpu.CompilerParams(vmem_limit_bytes=24 * 1024 * 1024),
    )(own_rows, here, near, far, occ_energy, window_start, vir_energy[None, :])


def exchange_kernel(
    n_cycle, n_group, inner, halves, lanes, step_rows,
    blocks_ref, dens_hbm, own_ref, int_ref, start_ref, aux_out, lag_out,
    dens_ref, own_block, load_sem, dens_recv, dens_f32, pair_send, pair_recv, aux_sum, plane_send, plane_recv, plane_sum,
    line_send, line_recv, int_vmem, lag_acc, lag_send, lag_recv,
    int_sem, dens_ss, dens_rs, pair_ss, pair_rs, plane_ss, plane_rs, line_ss, line_rs,
    lag_ss, lag_rs,
):
    cyc = lax.axis_index("occ")
    grp = lax.axis_index("grp")
    n_dev = n_cycle * n_group
    me = cyc * n_group + grp
    outer = n_cycle // inner
    seat = lax.rem(cyc, inner)
    plane = cyc // inner
    tall_block = blocks_ref.shape[2]
    half_rows = lanes * tall_block
    rows = halves * half_rows
    depth = step_rows * lanes * 128
    n_steps = halves * tall_block // step_rows

    def int_copy(k):
        part = pl.ds(pl.multiple_of(k * depth, depth), depth)
        return pltpu.make_async_copy(int_ref.at[part], int_vmem.at[part], int_sem.at[k])

    dens_load = pltpu.make_async_copy(dens_hbm, dens_ref, load_sem.at[0])
    block_load = pltpu.make_async_copy(blocks_ref.at[me], own_block, load_sem.at[1])
    dens_load.start()
    block_load.start()
    barrier = pltpu.get_barrier_semaphore()

    @pl.loop(1, n_dev)
    def _(s):
        d = lax.rem(me + s, n_dev)
        pl.semaphore_signal(
            barrier, inc=1, device_id=(d // n_group, lax.rem(d, n_group)), device_id_type=MESH
        )

    @pl.loop(0, n_steps)
    def _(k):
        int_copy(k).start()

    pl.semaphore_wait(barrier, n_dev - 1)

    def dens_copy(h, s):
        d = lax.rem(me + s, n_dev)
        part = pl.ds(h * lanes, lanes)
        return pltpu.make_async_remote_copy(
            src_ref=blocks_ref.at[d, part], dst_ref=dens_recv.at[s - 1, part],
            send_sem=dens_ss.at[h, s - 1], recv_sem=dens_rs.at[h, s - 1],
            device_id=(d // n_group, lax.rem(d, n_group)), device_id_type=MESH,
        )

    def pair_copy(s):
        return pltpu.make_async_remote_copy(
            src_ref=pair_send.at[s - 1], dst_ref=pair_recv.at[s - 1],
            send_sem=pair_ss.at[s - 1], recv_sem=pair_rs.at[s - 1],
            device_id=(cyc, lax.rem(grp + s, n_group)), device_id_type=MESH,
        )

    def plane_copy(s):
        q = lax.rem(seat + s, inner)
        return pltpu.make_async_remote_copy(
            src_ref=plane_send.at[s - 1], dst_ref=plane_recv.at[s - 1],
            send_sem=plane_ss.at[s - 1], recv_sem=plane_rs.at[s - 1],
            device_id=(plane * inner + q, grp), device_id_type=MESH,
        )

    def line_copy(s):
        z = lax.rem(plane + s, outer)
        return pltpu.make_async_remote_copy(
            src_ref=line_send.at[s - 1], dst_ref=line_recv.at[s - 1],
            send_sem=line_ss.at[s - 1], recv_sem=line_rs.at[s - 1],
            device_id=(z * inner + seat, grp), device_id_type=MESH,
        )

    def lag_copy(s):
        d = lax.rem(me + s, n_dev)
        return pltpu.make_async_remote_copy(
            src_ref=lag_send.at[d], dst_ref=lag_recv.at[s - 1],
            send_sem=lag_ss.at[s - 1], recv_sem=lag_rs.at[s - 1],
            device_id=(d // n_group, lax.rem(d, n_group)), device_id_type=MESH,
        )

    for h in range(halves):
        @pl.loop(1, n_dev)
        def _(s):
            dens_copy(h, s).start()

    def own_part(g):
        width = aux_out.shape[1]
        if len(own_ref.shape) == 3:
            return own_ref[g]
        return own_ref[:, pl.ds(pl.multiple_of(g * width, 128), width)]

    def aux_columns(g):
        return lax.dot_general(
            dens_ref[...], own_part(g), (((0,), (0,)), ((), ())),
            preferred_element_type=jnp.float32,
        ).reshape(aux_sum.shape)

    dens_load.wait()
    block_load.wait()
    for s in range(1, n_group):
        pair_send[s - 1] = aux_columns(lax.rem(grp + s, n_group))
        pair_copy(s).start()
    aux_sum[...] = aux_columns(grp)
    for s in range(1, n_group):
        pair_copy(s).wait_recv()

        @pl.loop(0, n_cycle)
        def _(o):
            aux_sum[o] += pair_recv[s - 1, o]

    for s in range(1, inner):
        q = lax.rem(seat + s, inner)

        @pl.loop(0, outer)
        def _(z):
            plane_send[s - 1, z] = aux_sum[z * inner + q].astype(plane_send.dtype)

        plane_copy(s).start()

    def take_half(h):
        part = pl.ds(h * lanes, lanes)
        own_at = pl.ds(me * rows + h * half_rows, half_rows)
        dens_f32[own_at, :] = own_block[part].astype(jnp.float32).reshape(half_rows, 128)

        @pl.loop(1, n_dev)
        def _(s):
            dens_copy(h, s).wait_recv()
            source = lax.rem(me - s + n_dev, n_dev)
            at = pl.ds(source * rows + h * half_rows, half_rows)
            block = dens_recv[s - 1, part].astype(jnp.float32)
            dens_f32[at, :] = block.reshape(half_rows, 128)

        steps = n_steps // halves

        @pl.loop(h * steps, (h + 1) * steps)
        def _(k):
            int_copy(k).wait()
            pieces = [
                dens_f32[
                    pl.ds(
                        h * half_rows + c * tall_block + (k - h * steps) * step_rows + j,
                        n_dev, stride=rows,
                    ), :
                ]
                for j in range(step_rows) for c in range(lanes)
            ]
            left = jnp.concatenate(pieces, axis=1).astype(jnp.bfloat16)
            at = pl.ds(pl.multiple_of(k * depth, depth), depth)
            lag_acc[...] += jnp.dot(left, int_vmem[at, :], preferred_element_type=jnp.float32)

    lag_acc[...] = jnp.zeros_like(lag_acc)
    for h in range(halves - 1):
        take_half(h)

    for s in range(1, inner):
        plane_copy(s).wait_recv()

    @pl.loop(0, outer)
    def _(z):
        block = aux_sum[z * inner + seat]
        for s in range(1, inner):
            block = block + plane_recv[s - 1, z].astype(jnp.float32)
        plane_sum[z] = block

    for s in range(1, outer):
        line_send[s - 1] = plane_sum[lax.rem(plane + s, outer)].astype(line_send.dtype)
        line_copy(s).start()

    take_half(halves - 1)

    device = lax.broadcasted_iota(jnp.int32, (n_dev, n_dev), 1)
    place, group = work_of(device // n_group, device % n_group, n_cycle, n_group)
    place = place + lax.rem(start_ref[0], n_cycle)
    place = jnp.where(place >= n_cycle, place - n_cycle, place)
    orbital = lax.broadcasted_iota(jnp.int32, (n_dev, n_dev), 0)
    chosen = jnp.where(orbital == place * n_group + group, 1.0, 0.0)
    lag_acc[...] = jnp.dot(
        chosen, lag_acc[...], preferred_element_type=jnp.float32, precision=lax.Precision.HIGHEST
    )

    orb_block = lag_out.shape[1]
    for o in range(n_cycle):
        for g in range(n_group):
            lag_send[o * n_group + g] = lag_acc[
                o * n_group:(o + 1) * n_group, g * orb_block:(g + 1) * orb_block
            ]

    @pl.loop(1, n_dev)
    def _(s):
        lag_copy(s).start()

    aux_total = plane_sum[plane]
    for s in range(1, outer):
        line_copy(s).wait_recv()
        aux_total = aux_total + line_recv[s - 1].astype(jnp.float32)
    aux_out[...] = aux_total

    lag_out[...] = lag_send[me]

    @pl.loop(1, n_dev)
    def _(s):
        lag_copy(s).wait_recv()
        lag_out[...] += lag_recv[s - 1]

    for s in range(1, n_group):
        pair_copy(s).wait_send()
    for s in range(1, inner):
        plane_copy(s).wait_send()
    for s in range(1, outer):
        line_copy(s).wait_send()

    @pl.loop(1, n_dev)
    def _(s):
        for h in range(halves):
            dens_copy(h, s).wait_send()
        lag_copy(s).wait_send()


def exchange(n_cycle, n_group, dens_blocks, density, own_columns, int_rows, window_start):
    n_dev = dens_blocks.shape[0]
    n_vir, n_aux = density.shape
    row_block = n_aux // n_cycle
    col_block = n_aux // n_group
    depth, n_orb = int_rows.shape
    orb_block = n_orb // n_group
    _, _, _, lanes, halves, tall_block = block_plan(n_vir, n_aux, n_cycle, n_group)
    step_rows = 2 if tall_block % 2 == 0 else 1
    rows = halves * lanes * tall_block
    inner = 4 if n_cycle % 4 == 0 else 1
    outer = n_cycle // inner
    tile = (row_block, col_block)
    anywhere = pl.BlockSpec(memory_space=pl.ANY)
    vmem = pl.BlockSpec(memory_space=pltpu.VMEM)
    dma = pltpu.SemaphoreType.DMA
    return pl.pallas_call(
        functools.partial(
            exchange_kernel, n_cycle, n_group, inner, halves, lanes, step_rows
        ),
        out_shape=(
            jax.ShapeDtypeStruct(tile, jnp.float32),
            jax.ShapeDtypeStruct((n_group, orb_block), jnp.float32),
        ),
        in_specs=[anywhere, anywhere, vmem, anywhere, pl.BlockSpec(memory_space=pltpu.SMEM)],
        out_specs=(vmem, vmem),
        scratch_shapes=[
            pltpu.VMEM((n_vir, n_aux), jnp.bfloat16),
            pltpu.VMEM(dens_blocks.shape[1:], jnp.bfloat16),
            dma((2,)),
            pltpu.VMEM((n_dev - 1,) + dens_blocks.shape[1:], jnp.bfloat16),
            pltpu.VMEM((n_dev * rows, 128), jnp.float32),
            pltpu.VMEM((n_group - 1, n_cycle) + tile, jnp.float32),
            pltpu.VMEM((n_group - 1, n_cycle) + tile, jnp.float32),
            pltpu.VMEM((n_cycle,) + tile, jnp.float32),
            pltpu.VMEM((inner - 1, outer) + tile, jnp.bfloat16),
            pltpu.VMEM((inner - 1, outer) + tile, jnp.bfloat16),
            pltpu.VMEM((outer,) + tile, jnp.float32),
            pltpu.VMEM((outer - 1,) + tile, jnp.bfloat16),
            pltpu.VMEM((outer - 1,) + tile, jnp.bfloat16),
            pltpu.VMEM((depth, n_orb), jnp.bfloat16),
            pltpu.VMEM((n_dev, n_orb), jnp.float32),
            pltpu.VMEM((n_dev, n_group, orb_block), jnp.float32),
            pltpu.VMEM((n_dev - 1, n_group, orb_block), jnp.float32),
            dma((halves * tall_block // step_rows,)),
            dma((halves, n_dev - 1)), dma((halves, n_dev - 1)),
            dma((n_group - 1,)), dma((n_group - 1,)),
            dma((inner - 1,)), dma((inner - 1,)),
            dma((outer - 1,)), dma((outer - 1,)),
            dma((n_dev - 1,)), dma((n_dev - 1,)),
        ],
        compiler_params=pltpu.CompilerParams(
            collective_id=1, has_side_effects=True, vmem_limit_bytes=42 * 1024 * 1024
        ),
    )(dens_blocks, density, own_columns, int_rows, window_start)


def local(b_factors, occ_energy, vir_energy, integrals, window_start):
    n_cycle = lax.axis_size("occ")
    n_group = lax.axis_size("grp")
    offset = jnp.mod(window_start[0], n_cycle)
    own_rows = b_factors[0]
    n_vir, n_aux = own_rows.shape

    def gather(by, x):
        return (spread(x, by), *neighbours(n_cycle, n_group, x))

    work_rows, here, near, far = lax.switch(
        offset, [functools.partial(gather, by) for by in range(n_cycle)], own_rows
    )
    density, dens_blocks = pair_densities(
        n_cycle, n_group, work_rows, here, near, far, occ_energy, vir_energy, window_start
    )
    col_block = n_aux // n_group
    own_columns = work_rows
    if col_block % 128:
        own_columns = work_rows.reshape(n_vir, n_group, col_block).transpose(1, 0, 2)
    int_rows = integrals.reshape(-1, integrals.shape[2])
    return exchange(n_cycle, n_group, dens_blocks, density, own_columns, int_rows, window_start)


def solution(mesh):
    placed = (P(("occ", "grp"), None, None), P(), P(), P("grp", "occ", None), P())
    return jax.shard_map(
        local,
        mesh=mesh,
        in_specs=placed,
        out_specs=(P("occ", "grp"), P("occ", "grp")),
        check_vma=False,
    )
```

```python
import functools
import math

import jax
import jax.numpy as jnp
from jax import lax
from jax.experimental import pallas as pl
from jax.experimental.pallas import tpu as pltpu
from jax.sharding import PartitionSpec as P

MESH = pl.DeviceIdType.MESH
SHIFTS = 3


def work_of(cyc, grp, n_cycle, n_group):
    return cyc - cyc % 2 + grp % 2, grp - grp % 2 + cyc % 2


def spread(x, by):
    n_cycle, n_group = lax.axis_size("occ"), lax.axis_size("grp")
    pairs = []
    for cyc in range(n_cycle):
        for grp in range(n_group):
            pos, group = work_of(cyc, grp, n_cycle, n_group)
            pairs.append((((pos + by) % n_cycle) * n_group + group, cyc * n_group + grp))
    return lax.ppermute(x, ("occ", "grp"), pairs)


def block_plan(n_vir, n_aux, n_cycle, n_group):
    aux_local, vir_local = n_aux // n_cycle, n_vir // n_group
    joined = 128 // math.gcd(aux_local, 128)
    lanes = joined * aux_local // 128
    halves = 2 if vir_local % (32 * joined) == 0 else 1
    return aux_local, vir_local, joined, lanes, halves, vir_local // joined // halves


def neighbour_kernel(
    n_cycle, n_group, chunks,
    own, blocks, hop, copy_sem, swap_ss, swap_rs, out_ss, hop_rs, fwd_ss, far_rs, near_ss, near_rs,
):
    cyc = lax.axis_index("occ")
    grp = lax.axis_index("grp")
    x, y, core = lax.rem(cyc, 2), lax.rem(cyc // 2, 2), lax.rem(grp, 2)
    n_vir = own.shape[0]
    size = n_vir // chunks
    half = chunks // 2
    here, near, far = (blocks.at[pl.ds(t * n_vir, n_vir)] for t in range(SHIFTS))
    diagonal = (cyc + 1 - 2 * x, grp + 1 - 2 * core)
    twin = (cyc, grp + 1 - 2 * core)
    y_mate = (cyc + 2 - 4 * y, grp)
    above = (lax.rem(cyc + 4, n_cycle), grp)
    below = (lax.rem(cyc + n_cycle - 4, n_cycle), grp)
    barrier = pltpu.get_barrier_semaphore()
    for other in (twin, y_mate, below):
        pl.semaphore_signal(barrier, inc=1, device_id=other, device_id_type=MESH)

    @pl.when(x != core)
    def _():
        pl.semaphore_signal(barrier, inc=1, device_id=diagonal, device_id_type=MESH)

    pl.semaphore_wait(barrier, 3 + lax.rem(x + core, 2))

    def part(c):
        return pl.ds(c * size, size)

    def remote(src, dst, send_sem, recv_sem, to):
        return pltpu.make_async_remote_copy(
            src_ref=src, dst_ref=dst, send_sem=send_sem, recv_sem=recv_sem,
            device_id=to, device_id_type=MESH,
        )

    def swap_copy(c):
        return remote(own.at[part(c)], here.at[part(c)], swap_ss.at[c], swap_rs.at[c], diagonal)

    def near_copy(c, source):
        return remote(source.at[part(c)], near.at[part(c)], near_ss.at[c], near_rs.at[c], twin)

    def direct_copy(c, source):
        return remote(source.at[part(c)], far.at[part(c)], out_ss.at[c], far_rs.at[c], y_mate)

    def hop_copy(c, source):
        return remote(
            source.at[part(c)], hop.at[part(c % half)], out_ss.at[c], hop_rs.at[c % half],
            y_mate if c < half else above,
        )

    def up_copy(c):
        return remote(hop.at[part(c)], far.at[part(c)], fwd_ss.at[c], far_rs.at[c], above)

    def across_copy(c):
        return remote(
            hop.at[part(c)], far.at[part(c + half)], fwd_ss.at[c], far_rs.at[c + half], y_mate
        )

    def pass_on(c, source):
        @pl.when(y == 0)
        def _():
            direct_copy(c, source).start()

        @pl.when(y == 1)
        def _():
            hop_copy(c, source).start()

        @pl.when(core == 0)
        def _():
            near_copy(c, source).start()

    order = [c // 2 + half * (c % 2) for c in range(chunks)]
    keep = pltpu.make_async_copy(own, here, copy_sem)

    @pl.when(x == core)
    def _():
        for c in order:
            pass_on(c, own)
        keep.start()

    @pl.when(x != core)
    def _():
        for c in order:
            swap_copy(c).start()
        for c in order:
            swap_copy(c).wait_recv()
            pass_on(c, here)

    for c in range(half):
        hop_copy(c, own).wait_recv()

        @pl.when(y == 0)
        def _():
            up_copy(c).start()

        @pl.when(y == 1)
        def _():
            across_copy(c).start()

    for c in order:
        direct_copy(c, own).wait_recv()

        @pl.when(core == 1)
        def _():
            near_copy(c, far).start()

    for c in range(chunks):
        near_copy(c, far).wait_recv()
        near_copy(c, far).wait_send()
        direct_copy(c, own).wait_send()
    for c in range(half):
        up_copy(c).wait_send()

    @pl.when(x == core)
    def _():
        keep.wait()

    @pl.when(x != core)
    def _():
        for c in range(chunks):
            swap_copy(c).wait_send()


def neighbours(n_cycle, n_group, own_rows):
    n_vir, n_aux = own_rows.shape
    chunks = 8
    dma = pltpu.SemaphoreType.DMA
    anywhere = pl.BlockSpec(memory_space=pl.ANY)
    return pl.pallas_call(
        functools.partial(neighbour_kernel, n_cycle, n_group, chunks),
        out_shape=jax.ShapeDtypeStruct((SHIFTS * n_vir, n_aux), own_rows.dtype),
        in_specs=[anywhere],
        out_specs=anywhere,
        scratch_shapes=[
            pltpu.VMEM((n_vir // 2, n_aux), own_rows.dtype), dma,
            dma((chunks,)), dma((chunks,)), dma((chunks,)), dma((chunks // 2,)),
            dma((chunks // 2,)), dma((chunks,)), dma((chunks,)), dma((chunks,)),
        ],
        compiler_params=pltpu.CompilerParams(
            collective_id=0, has_side_effects=True, vmem_limit_bytes=4 * 1024 * 1024
        ),
        cost_estimate=pl.CostEstimate(
            flops=0, bytes_accessed=60 * n_vir * n_aux, transcendentals=0
        ),
    )(own_rows)


def window_kernel(
    n_cycle, n_group, inner, halves, lanes, joined, step_rows,
    own_hbm, columns_ref, others_ref, int_ref, energy_ref, start_ref, vir_row_ref, aux_out, lag_out,
    own_ref, dens_ref, blocks_ref, stage, vir_col_ref, load_sem, dens_recv, dens_f32, pair_send, pair_recv, aux_sum, plane_send, plane_recv, plane_sum,
    line_send, line_recv, int_vmem, lag_acc, lag_send, lag_recv,
    int_sem, dens_ss, dens_rs, pair_ss, pair_rs, plane_ss, plane_rs, line_ss, line_rs,
    lag_ss, lag_rs,
):
    cyc = lax.axis_index("occ")
    grp = lax.axis_index("grp")
    n_dev = n_cycle * n_group
    me = cyc * n_group + grp
    outer = n_cycle // inner
    seat = lax.rem(cyc, inner)
    plane = cyc // inner
    tall_block = blocks_ref.shape[2]
    half_rows = lanes * tall_block
    rows = halves * half_rows
    depth = step_rows * lanes * 128
    n_steps = halves * tall_block // step_rows

    def int_copy(k):
        part = pl.ds(pl.multiple_of(k * depth, depth), depth)
        return pltpu.make_async_copy(int_ref.at[part], int_vmem.at[part], int_sem.at[k])

    own_load = pltpu.make_async_copy(own_hbm, own_ref, load_sem)
    own_load.start()
    barrier = pltpu.get_barrier_semaphore()

    @pl.loop(1, n_dev)
    def _(s):
        d = lax.rem(me + s, n_dev)
        pl.semaphore_signal(
            barrier, inc=1, device_id=(d // n_group, lax.rem(d, n_group)), device_id_type=MESH
        )

    @pl.loop(0, n_steps)
    def _(k):
        int_copy(k).start()

    def dens_copy(h, s):
        d = lax.rem(me + s, n_dev)
        part = pl.ds(h * lanes, lanes)
        return pltpu.make_async_remote_copy(
            src_ref=blocks_ref.at[d, part], dst_ref=dens_recv.at[s - 1, part],
            send_sem=dens_ss.at[h, s - 1], recv_sem=dens_rs.at[h, s - 1],
            device_id=(d // n_group, lax.rem(d, n_group)), device_id_type=MESH,
        )

    def pair_copy(s):
        return pltpu.make_async_remote_copy(
            src_ref=pair_send.at[s - 1], dst_ref=pair_recv.at[s - 1],
            send_sem=pair_ss.at[s - 1], recv_sem=pair_rs.at[s - 1],
            device_id=(cyc, lax.rem(grp + s, n_group)), device_id_type=MESH,
        )

    def plane_copy(s):
        q = lax.rem(seat + s, inner)
        return pltpu.make_async_remote_copy(
            src_ref=plane_send.at[s - 1], dst_ref=plane_recv.at[s - 1],
            send_sem=plane_ss.at[s - 1], recv_sem=plane_rs.at[s - 1],
            device_id=(plane * inner + q, grp), device_id_type=MESH,
        )

    def line_copy(s):
        z = lax.rem(plane + s, outer)
        return pltpu.make_async_remote_copy(
            src_ref=line_send.at[s - 1], dst_ref=line_recv.at[s - 1],
            send_sem=line_ss.at[s - 1], recv_sem=line_rs.at[s - 1],
            device_id=(z * inner + seat, grp), device_id_type=MESH,
        )

    def lag_copy(s):
        d = lax.rem(me + s, n_dev)
        return pltpu.make_async_remote_copy(
            src_ref=lag_send.at[d], dst_ref=lag_recv.at[s - 1],
            send_sem=lag_ss.at[s - 1], recv_sem=lag_rs.at[s - 1],
            device_id=(d // n_group, lax.rem(d, n_group)), device_id_type=MESH,
        )

    n_vir, n_aux = own_ref.shape
    vir_local, aux_local = n_vir // n_group, n_aux // n_cycle
    tall = joined * tall_block
    place, group = work_of(cyc, grp, n_cycle, n_group)
    shift = lax.rem(start_ref[0], n_cycle)
    own_energy = energy_ref[lax.rem(place + shift, n_cycle) * n_group + group]
    across = (((1,), (1,)), ((), ()))
    vir_col_ref[...] = jnp.broadcast_to(vir_row_ref[...], (128, n_vir)).T

    def densities(h):
        at = [pl.ds(g * vir_local + h * tall, tall) for g in range(n_group)]
        mine = jnp.concatenate([own_ref[rows, :] for rows in at], axis=0)
        theirs = jnp.concatenate(
            [
                others_ref[pl.ds(t * n_vir + rows.start, tall), :]
                for t in range(SHIFTS) for rows in at
            ],
            axis=0,
        )
        straight = lax.dot_general(
            mine, others_ref[...], across, preferred_element_type=jnp.float32
        )
        crossed = lax.dot_general(
            theirs, own_ref[...], across, preferred_element_type=jnp.float32
        )
        levels = jnp.concatenate([vir_col_ref[rows, 0:1] for rows in at], axis=0) + vir_row_ref[...]
        deep = n_group * tall
        combined = []
        for t in range(SHIFTS):
            partner = lax.rem(place - t + n_cycle, n_cycle)
            energy = own_energy + energy_ref[partner * n_group + group]
            pair = 2.0 * straight[:, t * n_vir:(t + 1) * n_vir] - crossed[t * deep:(t + 1) * deep]
            combined.append((pair / (energy - levels)).astype(jnp.bfloat16))
        value = jnp.dot(
            jnp.concatenate(combined, axis=1), others_ref[...], preferred_element_type=jnp.float32
        )
        for b in range(n_aux // 128):
            stage[pl.ds(b * deep, deep), :] = value[:, b * 128:(b + 1) * 128]
        for g in range(n_group):
            dens_ref[at[g], :] = value[g * tall:(g + 1) * tall].astype(dens_ref.dtype)

        @pl.loop(0, n_group)
        def _(g):
            picked = [
                jnp.concatenate(
                    [
                        stage[pl.ds(b * deep + g * tall + j, tall_block, stride=joined), :]
                        for b in range(n_aux // 128)
                    ],
                    axis=1,
                )
                for j in range(joined)
            ]
            for o in range(n_cycle):
                wide = jnp.concatenate(
                    [piece[:, o * aux_local:(o + 1) * aux_local] for piece in picked], axis=1
                ).astype(blocks_ref.dtype)
                for c in range(lanes):
                    blocks_ref[o * n_group + g, h * lanes + c] = wide[:, c * 128:(c + 1) * 128]

    own_load.wait()
    for h in range(halves):
        densities(h)
        if h == 0:
            pl.semaphore_wait(barrier, n_dev - 1)

        @pl.loop(1, n_dev)
        def _(s):
            dens_copy(h, s).start()

    def own_part(g):
        if columns_ref is not None:
            return columns_ref[g]
        width = aux_out.shape[1]
        return own_ref[:, pl.ds(pl.multiple_of(g * width, 128), width)]

    def aux_columns(g):
        return lax.dot_general(
            dens_ref[...], own_part(g), (((0,), (0,)), ((), ())),
            preferred_element_type=jnp.float32,
        ).reshape(aux_sum.shape)

    for s in range(1, n_group):
        pair_send[s - 1] = aux_columns(lax.rem(grp + s, n_group))
        pair_copy(s).start()
    aux_sum[...] = aux_columns(grp)
    for s in range(1, n_group):
        pair_copy(s).wait_recv()

        @pl.loop(0, n_cycle)
        def _(o):
            aux_sum[o] += pair_recv[s - 1, o]

    for s in range(1, inner):
        q = lax.rem(seat + s, inner)

        @pl.loop(0, outer)
        def _(z):
            plane_send[s - 1, z] = aux_sum[z * inner + q].astype(plane_send.dtype)

        plane_copy(s).start()

    def take_half(h):
        part = pl.ds(h * lanes, lanes)
        own_at = pl.ds(me * rows + h * half_rows, half_rows)
        dens_f32[own_at, :] = blocks_ref[me, part].astype(jnp.float32).reshape(half_rows, 128)

        @pl.loop(1, n_dev)
        def _(s):
            dens_copy(h, s).wait_recv()
            source = lax.rem(me - s + n_dev, n_dev)
            at = pl.ds(source * rows + h * half_rows, half_rows)
            block = dens_recv[s - 1, part].astype(jnp.float32)
            dens_f32[at, :] = block.reshape(half_rows, 128)

        steps = n_steps // halves

        @pl.loop(h * steps, (h + 1) * steps)
        def _(k):
            int_copy(k).wait()
            pieces = [
                dens_f32[
                    pl.ds(
                        h * half_rows + c * tall_block + (k - h * steps) * step_rows + j,
                        n_dev, stride=rows,
                    ), :
                ]
                for j in range(step_rows) for c in range(lanes)
            ]
            left = jnp.concatenate(pieces, axis=1).astype(jnp.bfloat16)
            at = pl.ds(pl.multiple_of(k * depth, depth), depth)
            lag_acc[...] += jnp.dot(left, int_vmem[at, :], preferred_element_type=jnp.float32)

    lag_acc[...] = jnp.zeros_like(lag_acc)
    for h in range(halves - 1):
        take_half(h)

    for s in range(1, inner):
        plane_copy(s).wait_recv()

    @pl.loop(0, outer)
    def _(z):
        block = aux_sum[z * inner + seat]
        for s in range(1, inner):
            block = block + plane_recv[s - 1, z].astype(jnp.float32)
        plane_sum[z] = block

    for s in range(1, outer):
        line_send[s - 1] = plane_sum[lax.rem(plane + s, outer)].astype(line_send.dtype)
        line_copy(s).start()

    take_half(halves - 1)

    device = lax.broadcasted_iota(jnp.int32, (n_dev, n_dev), 1)
    places, groups = work_of(device // n_group, device % n_group, n_cycle, n_group)
    places = places + shift
    places = jnp.where(places >= n_cycle, places - n_cycle, places)
    orbital = lax.broadcasted_iota(jnp.int32, (n_dev, n_dev), 0)
    chosen = jnp.where(orbital == places * n_group + groups, 1.0, 0.0)
    lag_acc[...] = jnp.dot(
        chosen, lag_acc[...], preferred_element_type=jnp.float32, precision=lax.Precision.HIGHEST
    )

    orb_block = lag_out.shape[1]
    for o in range(n_cycle):
        for g in range(n_group):
            lag_send[o * n_group + g] = lag_acc[
                o * n_group:(o + 1) * n_group, g * orb_block:(g + 1) * orb_block
            ]

    @pl.loop(1, n_dev)
    def _(s):
        lag_copy(s).start()

    aux_total = plane_sum[plane]
    for s in range(1, outer):
        line_copy(s).wait_recv()
        aux_total = aux_total + line_recv[s - 1].astype(jnp.float32)
    aux_out[...] = aux_total

    lag_out[...] = lag_send[me]

    @pl.loop(1, n_dev)
    def _(s):
        lag_copy(s).wait_recv()
        lag_out[...] += lag_recv[s - 1]

    for s in range(1, n_group):
        pair_copy(s).wait_send()
    for s in range(1, inner):
        plane_copy(s).wait_send()
    for s in range(1, outer):
        line_copy(s).wait_send()

    @pl.loop(1, n_dev)
    def _(s):
        for h in range(halves):
            dens_copy(h, s).wait_send()
        lag_copy(s).wait_send()


def window(n_cycle, n_group, work_rows, others, int_rows, occ_energy, vir_energy, window_start):
    n_dev = n_cycle * n_group
    n_vir, n_aux = work_rows.shape
    row_block = n_aux // n_cycle
    col_block = n_aux // n_group
    depth, n_orb = int_rows.shape
    orb_block = n_orb // n_group
    _, _, joined, lanes, halves, tall_block = block_plan(n_vir, n_aux, n_cycle, n_group)
    blocks = (halves * lanes, tall_block, 128)
    step_rows = 2 if tall_block % 2 == 0 else 1
    rows = halves * lanes * tall_block
    inner = 4 if n_cycle % 4 == 0 else 1
    outer = n_cycle // inner
    tile = (row_block, col_block)
    anywhere = pl.BlockSpec(memory_space=pl.ANY)
    vmem = pl.BlockSpec(memory_space=pltpu.VMEM)
    smem = pl.BlockSpec(memory_space=pltpu.SMEM)
    dma = pltpu.SemaphoreType.DMA
    columns = None
    if col_block % 128:
        columns = work_rows.reshape(n_vir, n_group, col_block).transpose(1, 0, 2)
    body = functools.partial(
        window_kernel, n_cycle, n_group, inner, halves, lanes, joined, step_rows
    )

    def kernel(own_hbm, *refs):
        if columns is None:
            body(own_hbm, None, *refs)
        else:
            body(own_hbm, *refs)

    return pl.pallas_call(
        kernel,
        out_shape=(
            jax.ShapeDtypeStruct(tile, jnp.float32),
            jax.ShapeDtypeStruct((n_group, orb_block), jnp.float32),
        ),
        in_specs=[anywhere] + [vmem] * (columns is not None) + [vmem, anywhere, smem, smem, vmem],
        out_specs=(vmem, vmem),
        scratch_shapes=[
            pltpu.VMEM((n_vir, n_aux), jnp.bfloat16),
            pltpu.VMEM((n_vir, n_aux), jnp.bfloat16),
            pltpu.VMEM((n_dev,) + blocks, jnp.bfloat16),
            pltpu.VMEM((n_aux // 128 * n_group * joined * tall_block, 128), jnp.float32),
            pltpu.VMEM((n_vir, 128), jnp.float32),
            dma,
            pltpu.VMEM((n_dev - 1,) + blocks, jnp.bfloat16),
            pltpu.VMEM((n_dev * rows, 128), jnp.float32),
            pltpu.VMEM((n_group - 1, n_cycle) + tile, jnp.float32),
            pltpu.VMEM((n_group - 1, n_cycle) + tile, jnp.float32),
            pltpu.VMEM((n_cycle,) + tile, jnp.float32),
            pltpu.VMEM((inner - 1, outer) + tile, jnp.bfloat16),
            pltpu.VMEM((inner - 1, outer) + tile, jnp.bfloat16),
            pltpu.VMEM((outer,) + tile, jnp.float32),
            pltpu.VMEM((outer - 1,) + tile, jnp.bfloat16),
            pltpu.VMEM((outer - 1,) + tile, jnp.bfloat16),
            pltpu.VMEM((depth, n_orb), jnp.bfloat16),
            pltpu.VMEM((n_dev, n_orb), jnp.float32),
            pltpu.VMEM((n_dev, n_group, orb_block), jnp.float32),
            pltpu.VMEM((n_dev - 1, n_group, orb_block), jnp.float32),
            dma((halves * tall_block // step_rows,)),
            dma((halves, n_dev - 1)), dma((halves, n_dev - 1)),
            dma((n_group - 1,)), dma((n_group - 1,)),
            dma((inner - 1,)), dma((inner - 1,)),
            dma((outer - 1,)), dma((outer - 1,)),
            dma((n_dev - 1,)), dma((n_dev - 1,)),
        ],
        compiler_params=pltpu.CompilerParams(
            collective_id=1, has_side_effects=True, vmem_limit_bytes=44 * 1024 * 1024
        ),
    )(
        work_rows, *([] if columns is None else [columns]), others, int_rows, occ_energy,
        window_start, vir_energy[None, :],
    )


def local(b_factors, occ_energy, vir_energy, integrals, window_start):
    n_cycle = lax.axis_size("occ")
    n_group = lax.axis_size("grp")
    offset = jnp.mod(window_start[0], n_cycle)
    own_rows = b_factors[0]

    def gather(by, x):
        return spread(x, by), neighbours(n_cycle, n_group, x)

    work_rows, others = lax.switch(
        offset, [functools.partial(gather, by) for by in range(n_cycle)], own_rows
    )
    int_rows = integrals.reshape(-1, integrals.shape[2])
    return window(
        n_cycle, n_group, work_rows, others, int_rows, occ_energy, vir_energy, window_start
    )


def solution(mesh):
    placed = (P(("occ", "grp"), None, None), P(), P(), P("grp", "occ", None), P())
    return jax.shard_map(
        local,
        mesh=mesh,
        in_specs=placed,
        out_specs=(P("occ", "grp"), P("occ", "grp")),
        check_vma=False,
    )
```

```python
import functools
import math

import jax
import jax.numpy as jnp
from jax import lax
from jax.experimental import pallas as pl
from jax.experimental.pallas import tpu as pltpu
from jax.sharding import PartitionSpec as P

MESH = pl.DeviceIdType.MESH
SHIFTS = 3


def work_of(cyc, grp, n_cycle, n_group):
    return cyc - cyc % 2 + grp % 2, grp - grp % 2 + cyc % 2


def route_plan(n_cycle):
    def cost(by):
        planes = -(-min(by, n_cycle - by) // 4)
        return max(2 * planes + 1, 4 if by % 4 == 2 else 2)

    plan = []
    for s in range(n_cycle):
        later = (s + 2) % n_cycle
        plan.append((later, 1) if cost(later) < cost(s) else (s, -1))
    return plan


def block_plan(n_vir, n_aux, n_cycle, n_group):
    aux_local, vir_local = n_aux // n_cycle, n_vir // n_group
    joined = 128 // math.gcd(aux_local, 128)
    lanes = joined * aux_local // 128
    halves = 2 if vir_local % (32 * joined) == 0 else 1
    return aux_local, vir_local, joined, lanes, halves, vir_local // joined // halves


def gather_kernel(
    n_cycle, n_group, chunks, by, side,
    own, work, blocks, hop, copy_sem, swap_ss, swap_rs, out_ss, hop_rs, fwd_ss, far_rs, near_ss, near_rs,
    turn_ss, turn_rs,
):
    cyc = lax.axis_index("occ")
    grp = lax.axis_index("grp")
    x, y, core = lax.rem(cyc, 2), lax.rem(cyc // 2, 2), lax.rem(grp, 2)
    n_vir = own.shape[0]
    size = n_vir // chunks
    half = chunks // 2
    here, near, far = (blocks.at[pl.ds(t * n_vir, n_vir)] for t in range(SHIFTS))
    diagonal = (cyc + 1 - 2 * x, grp + 1 - 2 * core)
    twin = (cyc, grp + 1 - 2 * core)
    y_mate = (cyc + 2 - 4 * y, grp)
    onward = (lax.rem(cyc + n_cycle - 4 * side, n_cycle), grp)
    back = (lax.rem(cyc + n_cycle + 4 * side, n_cycle), grp)
    first, lower = (y, core) if side < 0 else (1 - y, 1 - core)
    place, group = cyc - x + core, grp - core + x
    source = (lax.rem(place + by, n_cycle), group)
    goal = lax.rem(cyc + n_cycle - by, n_cycle)
    goal_x = lax.rem(goal, 2)
    goal = (goal - goal_x + core, grp - core + goal_x)
    barrier = pltpu.get_barrier_semaphore()
    for other in (twin, y_mate, back) + ((source,) if by else ()):
        pl.semaphore_signal(barrier, inc=1, device_id=other, device_id_type=MESH)

    @pl.when(x != core)
    def _():
        pl.semaphore_signal(barrier, inc=1, device_id=diagonal, device_id_type=MESH)

    pl.semaphore_wait(barrier, 3 + (by != 0) + lax.rem(x + core, 2))

    def part(c):
        return pl.ds(c * size, size)

    def remote(src, dst, send_sem, recv_sem, to):
        return pltpu.make_async_remote_copy(
            src_ref=src, dst_ref=dst, send_sem=send_sem, recv_sem=recv_sem,
            device_id=to, device_id_type=MESH,
        )

    def swap_copy(c):
        return remote(own.at[part(c)], here.at[part(c)], swap_ss.at[c], swap_rs.at[c], diagonal)

    def turn_copy(c):
        if by:
            return remote(own.at[part(c)], work.at[part(c)], turn_ss.at[c], turn_rs.at[c], goal)
        return pltpu.make_async_copy(here.at[part(c)], work.at[part(c)], turn_rs.at[c])

    def near_copy(c, source):
        return remote(source.at[part(c)], near.at[part(c)], near_ss.at[c], near_rs.at[c], twin)

    def direct_copy(c, source):
        return remote(source.at[part(c)], far.at[part(c)], out_ss.at[c], far_rs.at[c], y_mate)

    def hop_copy(c, source):
        return remote(
            source.at[part(c)], hop.at[part(c % half)], out_ss.at[c], hop_rs.at[c % half],
            y_mate if c < half else onward,
        )

    def onward_copy(c):
        return remote(hop.at[part(c)], far.at[part(c)], fwd_ss.at[c], far_rs.at[c], onward)

    def across_copy(c):
        return remote(
            hop.at[part(c)], far.at[part(c + half)], fwd_ss.at[c], far_rs.at[c + half], y_mate
        )

    def pass_on(c, source):
        @pl.when(first == 0)
        def _():
            direct_copy(c, source).start()

        @pl.when(first == 1)
        def _():
            hop_copy(c, source).start()

        @pl.when(lower == 0)
        def _():
            near_copy(c, source).start()

    order = [c // 2 + half * (c % 2) for c in range(chunks)]
    turns = iter(range(chunks) if by else ())

    def turn(count):
        for c in [c for _, c in zip(range(count), turns)]:
            turn_copy(c).start()

    keep = pltpu.make_async_copy(own, here, copy_sem)

    @pl.when(x == core)
    def _():
        for c in order:
            pass_on(c, own)
        keep.start()

    @pl.when(x != core)
    def _():
        for c in order:
            swap_copy(c).start()
        for c in order:
            swap_copy(c).wait_recv()
            pass_on(c, here)

    turn(2)
    for c in range(half):
        hop_copy(c, own).wait_recv()

        @pl.when(first == 0)
        def _():
            onward_copy(c).start()

        @pl.when(first == 1)
        def _():
            across_copy(c).start()

        turn(1)

    turn(chunks)

    @pl.when(x == core)
    def _():
        keep.wait()

    if not by:
        for c in range(chunks):
            turn_copy(c).start()

    for c in order:
        direct_copy(c, own).wait_recv()

        @pl.when(lower == 1)
        def _():
            near_copy(c, far).start()

    for c in range(chunks):
        near_copy(c, far).wait_recv()
        near_copy(c, far).wait_send()
        direct_copy(c, own).wait_send()
        if by:
            turn_copy(c).wait_recv()
            turn_copy(c).wait_send()
        else:
            turn_copy(c).wait()
    for c in range(half):
        onward_copy(c).wait_send()

    @pl.when(x != core)
    def _():
        for c in range(chunks):
            swap_copy(c).wait_send()


def gather(n_cycle, n_group, shift, by, side, own_rows):
    n_vir, n_aux = own_rows.shape
    chunks = 8
    dma = pltpu.SemaphoreType.DMA
    anywhere = pl.BlockSpec(memory_space=pl.ANY)
    return pl.pallas_call(
        functools.partial(gather_kernel, n_cycle, n_group, chunks, by, side),
        out_shape=(
            jax.ShapeDtypeStruct((n_vir, n_aux), own_rows.dtype),
            jax.ShapeDtypeStruct((SHIFTS * n_vir, n_aux), own_rows.dtype),
        ),
        in_specs=[anywhere],
        out_specs=(anywhere, anywhere),
        scratch_shapes=[
            pltpu.VMEM((n_vir // 2, n_aux), own_rows.dtype), dma,
            dma((chunks,)), dma((chunks,)), dma((chunks,)), dma((chunks // 2,)),
            dma((chunks // 2,)), dma((chunks,)), dma((chunks,)), dma((chunks,)),
            dma((chunks,)), dma((chunks,)),
        ],
        compiler_params=pltpu.CompilerParams(
            collective_id=1 + shift, has_side_effects=True, vmem_limit_bytes=4 * 1024 * 1024
        ),
    )(own_rows)


def window_kernel(
    n_cycle, n_group, inner, halves, lanes, joined, step_rows,
    own_hbm, columns_ref, others_ref, int_ref, energy_ref, start_ref, vir_row_ref, aux_out, lag_out,
    own_ref, dens_ref, blocks_ref, stage, vir_col_ref, load_sem, dens_recv, dens_f32, pair_send, pair_recv, aux_sum, plane_send, plane_recv, plane_sum,
    line_send, line_recv, int_vmem, lag_acc, lag_send, lag_recv,
    int_sem, dens_ss, dens_rs, pair_ss, pair_rs, plane_ss, plane_rs, line_ss, line_rs,
    lag_ss, lag_rs,
):
    cyc = lax.axis_index("occ")
    grp = lax.axis_index("grp")
    n_dev = n_cycle * n_group
    me = cyc * n_group + grp
    outer = n_cycle // inner
    seat = lax.rem(cyc, inner)
    plane = cyc // inner
    tall_block = blocks_ref.shape[2]
    half_rows = lanes * tall_block
    rows = halves * half_rows
    depth = step_rows * lanes * 128
    n_steps = halves * tall_block // step_rows

    def int_copy(k):
        part = pl.ds(pl.multiple_of(k * depth, depth), depth)
        return pltpu.make_async_copy(int_ref.at[part], int_vmem.at[part], int_sem.at[k])

    own_load = pltpu.make_async_copy(own_hbm, own_ref, load_sem)
    own_load.start()
    barrier = pltpu.get_barrier_semaphore()

    @pl.loop(1, n_dev)
    def _(s):
        d = lax.rem(me + s, n_dev)
        pl.semaphore_signal(
            barrier, inc=1, device_id=(d // n_group, lax.rem(d, n_group)), device_id_type=MESH
        )

    @pl.loop(0, n_steps)
    def _(k):
        int_copy(k).start()

    def dens_copy(h, s):
        d = lax.rem(me + s, n_dev)
        part = pl.ds(h * lanes, lanes)
        return pltpu.make_async_remote_copy(
            src_ref=blocks_ref.at[d, part], dst_ref=dens_recv.at[s - 1, part],
            send_sem=dens_ss.at[h, s - 1], recv_sem=dens_rs.at[h, s - 1],
            device_id=(d // n_group, lax.rem(d, n_group)), device_id_type=MESH,
        )

    def pair_copy(s):
        return pltpu.make_async_remote_copy(
            src_ref=pair_send.at[s - 1], dst_ref=pair_recv.at[s - 1],
            send_sem=pair_ss.at[s - 1], recv_sem=pair_rs.at[s - 1],
            device_id=(cyc, lax.rem(grp + s, n_group)), device_id_type=MESH,
        )

    def plane_copy(s):
        q = lax.rem(seat + s, inner)
        return pltpu.make_async_remote_copy(
            src_ref=plane_send.at[s - 1], dst_ref=plane_recv.at[s - 1],
            send_sem=plane_ss.at[s - 1], recv_sem=plane_rs.at[s - 1],
            device_id=(plane * inner + q, grp), device_id_type=MESH,
        )

    def line_copy(s):
        z = lax.rem(plane + s, outer)
        return pltpu.make_async_remote_copy(
            src_ref=line_send.at[s - 1], dst_ref=line_recv.at[s - 1],
            send_sem=line_ss.at[s - 1], recv_sem=line_rs.at[s - 1],
            device_id=(z * inner + seat, grp), device_id_type=MESH,
        )

    def lag_copy(s):
        d = lax.rem(me + s, n_dev)
        return pltpu.make_async_remote_copy(
            src_ref=lag_send.at[d], dst_ref=lag_recv.at[s - 1],
            send_sem=lag_ss.at[s - 1], recv_sem=lag_rs.at[s - 1],
            device_id=(d // n_group, lax.rem(d, n_group)), device_id_type=MESH,
        )

    n_vir, n_aux = own_ref.shape
    vir_local, aux_local = n_vir // n_group, n_aux // n_cycle
    tall = joined * tall_block
    place, group = work_of(cyc, grp, n_cycle, n_group)
    shift = lax.rem(start_ref[0], n_cycle)
    by, side = 0, -1
    for s, (turned, on) in enumerate(route_plan(n_cycle)):
        by = jnp.where(shift == s, turned, by)
        side = jnp.where(shift == s, on, side)
    own_energy = energy_ref[lax.rem(place + by, n_cycle) * n_group + group]
    across = (((1,), (1,)), ((), ()))
    vir_col_ref[...] = jnp.broadcast_to(vir_row_ref[...], (128, n_vir)).T

    def densities(h):
        at = [pl.ds(g * vir_local + h * tall, tall) for g in range(n_group)]
        mine = jnp.concatenate([own_ref[rows, :] for rows in at], axis=0)
        theirs = jnp.concatenate(
            [
                others_ref[pl.ds(t * n_vir + rows.start, tall), :]
                for t in range(SHIFTS) for rows in at
            ],
            axis=0,
        )
        straight = lax.dot_general(
            mine, others_ref[...], across, preferred_element_type=jnp.float32
        )
        crossed = lax.dot_general(
            theirs, own_ref[...], across, preferred_element_type=jnp.float32
        )
        levels = jnp.concatenate([vir_col_ref[rows, 0:1] for rows in at], axis=0) + vir_row_ref[...]
        deep = n_group * tall
        combined = []
        for t in range(SHIFTS):
            partner = lax.rem(place + side * t + n_cycle, n_cycle)
            energy = own_energy + energy_ref[partner * n_group + group]
            pair = 2.0 * straight[:, t * n_vir:(t + 1) * n_vir] - crossed[t * deep:(t + 1) * deep]
            combined.append((pair / (energy - levels)).astype(jnp.bfloat16))
        value = jnp.dot(
            jnp.concatenate(combined, axis=1), others_ref[...], preferred_element_type=jnp.float32
        )
        for b in range(n_aux // 128):
            stage[pl.ds(b * deep, deep), :] = value[:, b * 128:(b + 1) * 128]
        for g in range(n_group):
            dens_ref[at[g], :] = value[g * tall:(g + 1) * tall].astype(dens_ref.dtype)

        @pl.loop(0, n_group)
        def _(g):
            picked = [
                jnp.concatenate(
                    [
                        stage[pl.ds(b * deep + g * tall + j, tall_block, stride=joined), :]
                        for b in range(n_aux // 128)
                    ],
                    axis=1,
                )
                for j in range(joined)
            ]
            for o in range(n_cycle):
                wide = jnp.concatenate(
                    [piece[:, o * aux_local:(o + 1) * aux_local] for piece in picked], axis=1
                ).astype(blocks_ref.dtype)
                for c in range(lanes):
                    blocks_ref[o * n_group + g, h * lanes + c] = wide[:, c * 128:(c + 1) * 128]

    own_load.wait()
    for h in range(halves):
        densities(h)
        if h == 0:
            pl.semaphore_wait(barrier, n_dev - 1)

        @pl.loop(1, n_dev)
        def _(s):
            dens_copy(h, s).start()

    def own_part(g):
        if columns_ref is not None:
            return columns_ref[g]
        width = aux_out.shape[1]
        return own_ref[:, pl.ds(pl.multiple_of(g * width, 128), width)]

    def aux_columns(g):
        return lax.dot_general(
            dens_ref[...], own_part(g), (((0,), (0,)), ((), ())),
            preferred_element_type=jnp.float32,
        ).reshape(aux_sum.shape)

    for s in range(1, n_group):
        pair_send[s - 1] = aux_columns(lax.rem(grp + s, n_group))
        pair_copy(s).start()
    aux_sum[...] = aux_columns(grp)
    for s in range(1, n_group):
        pair_copy(s).wait_recv()

        @pl.loop(0, n_cycle)
        def _(o):
            aux_sum[o] += pair_recv[s - 1, o]

    for s in range(1, inner):
        q = lax.rem(seat + s, inner)

        @pl.loop(0, outer)
        def _(z):
            plane_send[s - 1, z] = aux_sum[z * inner + q].astype(plane_send.dtype)

        plane_copy(s).start()

    def take_half(h):
        part = pl.ds(h * lanes, lanes)
        own_at = pl.ds(me * rows + h * half_rows, half_rows)
        dens_f32[own_at, :] = blocks_ref[me, part].astype(jnp.float32).reshape(half_rows, 128)

        @pl.loop(1, n_dev)
        def _(s):
            dens_copy(h, s).wait_recv()
            source = lax.rem(me - s + n_dev, n_dev)
            at = pl.ds(source * rows + h * half_rows, half_rows)
            block = dens_recv[s - 1, part].astype(jnp.float32)
            dens_f32[at, :] = block.reshape(half_rows, 128)

        steps = n_steps // halves

        @pl.loop(h * steps, (h + 1) * steps)
        def _(k):
            int_copy(k).wait()
            pieces = [
                dens_f32[
                    pl.ds(
                        h * half_rows + c * tall_block + (k - h * steps) * step_rows + j,
                        n_dev, stride=rows,
                    ), :
                ]
                for j in range(step_rows) for c in range(lanes)
            ]
            left = jnp.concatenate(pieces, axis=1).astype(jnp.bfloat16)
            at = pl.ds(pl.multiple_of(k * depth, depth), depth)
            lag_acc[...] += jnp.dot(left, int_vmem[at, :], preferred_element_type=jnp.float32)

    lag_acc[...] = jnp.zeros_like(lag_acc)
    for h in range(halves - 1):
        take_half(h)

    for s in range(1, inner):
        plane_copy(s).wait_recv()

    @pl.loop(0, outer)
    def _(z):
        block = aux_sum[z * inner + seat]
        for s in range(1, inner):
            block = block + plane_recv[s - 1, z].astype(jnp.float32)
        plane_sum[z] = block

    for s in range(1, outer):
        line_send[s - 1] = plane_sum[lax.rem(plane + s, outer)].astype(line_send.dtype)
        line_copy(s).start()

    take_half(halves - 1)

    device = lax.broadcasted_iota(jnp.int32, (n_dev, n_dev), 1)
    places, groups = work_of(device // n_group, device % n_group, n_cycle, n_group)
    places = places + by
    places = jnp.where(places >= n_cycle, places - n_cycle, places)
    orbital = lax.broadcasted_iota(jnp.int32, (n_dev, n_dev), 0)
    chosen = jnp.where(orbital == places * n_group + groups, 1.0, 0.0)
    lag_acc[...] = jnp.dot(
        chosen, lag_acc[...], preferred_element_type=jnp.float32, precision=lax.Precision.HIGHEST
    )

    orb_block = lag_out.shape[1]
    for o in range(n_cycle):
        for g in range(n_group):
            lag_send[o * n_group + g] = lag_acc[
                o * n_group:(o + 1) * n_group, g * orb_block:(g + 1) * orb_block
            ]

    @pl.loop(1, n_dev)
    def _(s):
        lag_copy(s).start()

    aux_total = plane_sum[plane]
    for s in range(1, outer):
        line_copy(s).wait_recv()
        aux_total = aux_total + line_recv[s - 1].astype(jnp.float32)
    aux_out[...] = aux_total

    lag_out[...] = lag_send[me]

    @pl.loop(1, n_dev)
    def _(s):
        lag_copy(s).wait_recv()
        lag_out[...] += lag_recv[s - 1]

    for s in range(1, n_group):
        pair_copy(s).wait_send()
    for s in range(1, inner):
        plane_copy(s).wait_send()
    for s in range(1, outer):
        line_copy(s).wait_send()

    @pl.loop(1, n_dev)
    def _(s):
        for h in range(halves):
            dens_copy(h, s).wait_send()
        lag_copy(s).wait_send()


def window(n_cycle, n_group, work_rows, others, int_rows, occ_energy, vir_energy, window_start):
    n_dev = n_cycle * n_group
    n_vir, n_aux = work_rows.shape
    row_block = n_aux // n_cycle
    col_block = n_aux // n_group
    depth, n_orb = int_rows.shape
    orb_block = n_orb // n_group
    _, _, joined, lanes, halves, tall_block = block_plan(n_vir, n_aux, n_cycle, n_group)
    blocks = (halves * lanes, tall_block, 128)
    step_rows = 2 if tall_block % 2 == 0 else 1
    rows = halves * lanes * tall_block
    inner = 4 if n_cycle % 4 == 0 else 1
    outer = n_cycle // inner
    tile = (row_block, col_block)
    anywhere = pl.BlockSpec(memory_space=pl.ANY)
    vmem = pl.BlockSpec(memory_space=pltpu.VMEM)
    smem = pl.BlockSpec(memory_space=pltpu.SMEM)
    dma = pltpu.SemaphoreType.DMA
    columns = None
    if col_block % 128:
        columns = work_rows.reshape(n_vir, n_group, col_block).transpose(1, 0, 2)
    body = functools.partial(
        window_kernel, n_cycle, n_group, inner, halves, lanes, joined, step_rows
    )

    def kernel(own_hbm, *refs):
        if columns is None:
            body(own_hbm, None, *refs)
        else:
            body(own_hbm, *refs)

    return pl.pallas_call(
        kernel,
        out_shape=(
            jax.ShapeDtypeStruct(tile, jnp.float32),
            jax.ShapeDtypeStruct((n_group, orb_block), jnp.float32),
        ),
        in_specs=[anywhere] + [vmem] * (columns is not None) + [vmem, anywhere, smem, smem, vmem],
        out_specs=(vmem, vmem),
        scratch_shapes=[
            pltpu.VMEM((n_vir, n_aux), jnp.bfloat16),
            pltpu.VMEM((n_vir, n_aux), jnp.bfloat16),
            pltpu.VMEM((n_dev,) + blocks, jnp.bfloat16),
            pltpu.VMEM((n_aux // 128 * n_group * joined * tall_block, 128), jnp.float32),
            pltpu.VMEM((n_vir, 128), jnp.float32),
            dma,
            pltpu.VMEM((n_dev - 1,) + blocks, jnp.bfloat16),
            pltpu.VMEM((n_dev * rows, 128), jnp.float32),
            pltpu.VMEM((n_group - 1, n_cycle) + tile, jnp.float32),
            pltpu.VMEM((n_group - 1, n_cycle) + tile, jnp.float32),
            pltpu.VMEM((n_cycle,) + tile, jnp.float32),
            pltpu.VMEM((inner - 1, outer) + tile, jnp.bfloat16),
            pltpu.VMEM((inner - 1, outer) + tile, jnp.bfloat16),
            pltpu.VMEM((outer,) + tile, jnp.float32),
            pltpu.VMEM((outer - 1,) + tile, jnp.bfloat16),
            pltpu.VMEM((outer - 1,) + tile, jnp.bfloat16),
            pltpu.VMEM((depth, n_orb), jnp.bfloat16),
            pltpu.VMEM((n_dev, n_orb), jnp.float32),
            pltpu.VMEM((n_dev, n_group, orb_block), jnp.float32),
            pltpu.VMEM((n_dev - 1, n_group, orb_block), jnp.float32),
            dma((halves * tall_block // step_rows,)),
            dma((halves, n_dev - 1)), dma((halves, n_dev - 1)),
            dma((n_group - 1,)), dma((n_group - 1,)),
            dma((inner - 1,)), dma((inner - 1,)),
            dma((outer - 1,)), dma((outer - 1,)),
            dma((n_dev - 1,)), dma((n_dev - 1,)),
        ],
        compiler_params=pltpu.CompilerParams(
            collective_id=0, has_side_effects=True, vmem_limit_bytes=44 * 1024 * 1024
        ),
    )(
        work_rows, *([] if columns is None else [columns]), others, int_rows, occ_energy,
        window_start, vir_energy[None, :],
    )


def local(b_factors, occ_energy, vir_energy, integrals, window_start):
    n_cycle = lax.axis_size("occ")
    n_group = lax.axis_size("grp")
    offset = jnp.mod(window_start[0], n_cycle)
    own_rows = b_factors[0]

    work_rows, others = lax.switch(
        offset,
        [
            functools.partial(gather, n_cycle, n_group, shift, by, side)
            for shift, (by, side) in enumerate(route_plan(n_cycle))
        ],
        own_rows,
    )
    int_rows = integrals.reshape(-1, integrals.shape[2])
    return window(
        n_cycle, n_group, work_rows, others, int_rows, occ_energy, vir_energy, window_start
    )


def solution(mesh):
    placed = (P(("occ", "grp"), None, None), P(), P(), P("grp", "occ", None), P())
    return jax.shard_map(
        local,
        mesh=mesh,
        in_specs=placed,
        out_specs=(P("occ", "grp"), P("occ", "grp")),
        check_vma=False,
    )
```

```python
import functools
import math

import jax
import jax.numpy as jnp
from jax import lax
from jax.experimental import pallas as pl
from jax.experimental.pallas import tpu as pltpu
from jax.sharding import PartitionSpec as P

MESH = pl.DeviceIdType.MESH
SHIFTS = 3


def work_of(cyc, grp, n_cycle, n_group):
    return cyc - cyc % 2 + grp % 2, grp - grp % 2 + cyc % 2


def route_plan(n_cycle):
    def cost(by):
        planes, rest = divmod(min(by, n_cycle - by), 4)
        z = planes + (0, 0.5 if planes else 1, 0.5 if planes else 1, 1)[rest] + 0.5
        y = (1, 1.5, 2, 1.5)[rest]
        return max(z, y), z

    plan = []
    for s in range(n_cycle):
        later = (s + 2) % n_cycle
        plan.append((later, 1) if cost(later) < cost(s) else (s, -1))
    return plan


def block_plan(n_vir, n_aux, n_cycle, n_group):
    aux_local, vir_local = n_aux // n_cycle, n_vir // n_group
    joined = 128 // math.gcd(aux_local, 128)
    lanes = joined * aux_local // 128
    halves = 2 if vir_local % (32 * joined) == 0 else 1
    return aux_local, vir_local, joined, lanes, halves, vir_local // joined // halves


def ferried(n_cycle, chunks, by):
    planes, rest = divmod(min(by, n_cycle - by), 4)
    return max(1, chunks // (2 * planes + 2)) if planes and rest in (1, 2) else 0


def gather_kernel(
    n_cycle, n_group, chunks, by, side,
    own, work, blocks, hop, copy_sem, swap_ss, swap_rs, out_ss, hop_rs, fwd_ss, far_rs, near_ss, near_rs,
    turn_ss, turn_rs, ferry, ferry_ss, ferry_rs,
):
    cyc = lax.axis_index("occ")
    grp = lax.axis_index("grp")
    x, y, core = lax.rem(cyc, 2), lax.rem(cyc // 2, 2), lax.rem(grp, 2)
    n_vir = own.shape[0]
    size = n_vir // chunks
    half = chunks // 2
    here, near, far = (blocks.at[pl.ds(t * n_vir, n_vir)] for t in range(SHIFTS))
    diagonal = (cyc + 1 - 2 * x, grp + 1 - 2 * core)
    twin = (cyc, grp + 1 - 2 * core)
    y_mate = (cyc + 2 - 4 * y, grp)
    onward = (lax.rem(cyc + n_cycle - 4 * side, n_cycle), grp)
    back = (lax.rem(cyc + n_cycle + 4 * side, n_cycle), grp)
    first, lower = (y, core) if side < 0 else (1 - y, 1 - core)
    place, group = cyc - x + core, grp - core + x
    source = (lax.rem(place + by, n_cycle), group)
    n_ferry = ferried(n_cycle, chunks, by)

    def goal_of(cyc):
        goal = lax.rem(cyc + n_cycle - by, n_cycle)
        goal_x = lax.rem(goal, 2)
        return (goal - goal_x + core, grp - core + goal_x)

    def climbs(cyc):
        seat = lax.rem(cyc, 4)
        if 2 * by <= n_cycle:
            return (seat < by % 4).astype(jnp.int32)
        return (seat >= by % 4).astype(jnp.int32)

    goal = goal_of(cyc)
    load, carry = climbs(cyc), climbs(y_mate[0])
    source_y = lax.rem(source[0] // 2, 2)
    source_mate = (source[0] + 2 - 4 * source_y, group)
    barrier = pltpu.get_barrier_semaphore()
    for other in (twin, y_mate, back) + ((source,) if by else ()):
        pl.semaphore_signal(barrier, inc=1, device_id=other, device_id_type=MESH)

    @pl.when(x != core)
    def _():
        pl.semaphore_signal(barrier, inc=1, device_id=diagonal, device_id_type=MESH)

    if n_ferry:
        @pl.when(climbs(source[0]) == 1)
        def _():
            pl.semaphore_signal(barrier, inc=1, device_id=source_mate, device_id_type=MESH)

    peers = 3 + (by != 0) + lax.rem(x + core, 2)
    pl.semaphore_wait(barrier, peers + carry if n_ferry else peers)

    def part(c):
        return pl.ds(c * size, size)

    def remote(src, dst, send_sem, recv_sem, to):
        return pltpu.make_async_remote_copy(
            src_ref=src, dst_ref=dst, send_sem=send_sem, recv_sem=recv_sem,
            device_id=to, device_id_type=MESH,
        )

    def swap_copy(c):
        return remote(own.at[part(c)], here.at[part(c)], swap_ss.at[c], swap_rs.at[c], diagonal)

    def turn_copy(c):
        if by:
            return remote(own.at[part(c)], work.at[part(c)], turn_ss.at[c], turn_rs.at[c], goal)
        return pltpu.make_async_copy(here.at[part(c)], work.at[part(c)], turn_rs.at[c])

    def ferry_copy(c):
        return remote(own.at[part(c)], ferry.at[part(c)], turn_ss.at[c], ferry_rs.at[c], y_mate)

    def carry_copy(c):
        return remote(
            ferry.at[part(c)], work.at[part(c)], ferry_ss.at[c], turn_rs.at[c], goal_of(y_mate[0])
        )

    def near_copy(c, source):
        return remote(source.at[part(c)], near.at[part(c)], near_ss.at[c], near_rs.at[c], twin)

    def direct_copy(c, source):
        return remote(source.at[part(c)], far.at[part(c)], out_ss.at[c], far_rs.at[c], y_mate)

    def hop_copy(c, source):
        return remote(
            source.at[part(c)], hop.at[part(c % half)], out_ss.at[c], hop_rs.at[c % half],
            y_mate if c < half else onward,
        )

    def onward_copy(c):
        return remote(hop.at[part(c)], far.at[part(c)], fwd_ss.at[c], far_rs.at[c], onward)

    def across_copy(c):
        return remote(
            hop.at[part(c)], far.at[part(c + half)], fwd_ss.at[c], far_rs.at[c + half], y_mate
        )

    def pass_on(c, source):
        @pl.when(first == 0)
        def _():
            direct_copy(c, source).start()

        @pl.when(first == 1)
        def _():
            hop_copy(c, source).start()

        @pl.when(lower == 0)
        def _():
            near_copy(c, source).start()

    order = [c // 2 + half * (c % 2) for c in range(chunks)]
    turns = iter(range(chunks) if by else ())

    def turn(count):
        for c in [c for _, c in zip(range(count), turns)]:
            if c < n_ferry:
                @pl.when(load == 0)
                def _():
                    turn_copy(c).start()

                @pl.when(load == 1)
                def _():
                    ferry_copy(c).start()
            else:
                turn_copy(c).start()

    keep = pltpu.make_async_copy(own, here, copy_sem)

    turn(2)

    @pl.when(x == core)
    def _():
        for c in order:
            pass_on(c, own)
        keep.start()

    @pl.when(x != core)
    def _():
        for c in order:
            swap_copy(c).start()
        for c in order:
            swap_copy(c).wait_recv()
            pass_on(c, here)

    turn(2)
    for c in range(n_ferry):
        @pl.when(carry == 1)
        def _():
            ferry_copy(c).wait_recv()
            carry_copy(c).start()

    for c in range(half):
        hop_copy(c, own).wait_recv()

        @pl.when(first == 0)
        def _():
            onward_copy(c).start()

        @pl.when(first == 1)
        def _():
            across_copy(c).start()

        turn(1)

    turn(chunks)

    @pl.when(x == core)
    def _():
        keep.wait()

    if not by:
        for c in range(chunks):
            turn_copy(c).start()

    for c in order:
        direct_copy(c, own).wait_recv()

        @pl.when(lower == 1)
        def _():
            near_copy(c, far).start()

    for c in range(chunks):
        near_copy(c, far).wait_recv()
        near_copy(c, far).wait_send()
        direct_copy(c, own).wait_send()
        if by:
            turn_copy(c).wait_recv()
            turn_copy(c).wait_send()
        else:
            turn_copy(c).wait()
    for c in range(half):
        onward_copy(c).wait_send()

    for c in range(n_ferry):
        @pl.when(carry == 1)
        def _():
            carry_copy(c).wait_send()

    @pl.when(x != core)
    def _():
        for c in range(chunks):
            swap_copy(c).wait_send()


def gather(n_cycle, n_group, shift, by, side, own_rows):
    n_vir, n_aux = own_rows.shape
    chunks = 8
    dma = pltpu.SemaphoreType.DMA
    anywhere = pl.BlockSpec(memory_space=pl.ANY)
    return pl.pallas_call(
        functools.partial(gather_kernel, n_cycle, n_group, chunks, by, side),
        out_shape=(
            jax.ShapeDtypeStruct((n_vir, n_aux), own_rows.dtype),
            jax.ShapeDtypeStruct((SHIFTS * n_vir, n_aux), own_rows.dtype),
        ),
        in_specs=[anywhere],
        out_specs=(anywhere, anywhere),
        scratch_shapes=[
            pltpu.VMEM((n_vir // 2, n_aux), own_rows.dtype), dma,
            dma((chunks,)), dma((chunks,)), dma((chunks,)), dma((chunks // 2,)),
            dma((chunks // 2,)), dma((chunks,)), dma((chunks,)), dma((chunks,)),
            dma((chunks,)), dma((chunks,)),
            pltpu.VMEM((n_vir // 2, n_aux), own_rows.dtype), dma((chunks // 2,)), dma((chunks // 2,)),
        ],
        compiler_params=pltpu.CompilerParams(
            collective_id=1 + shift, has_side_effects=True, vmem_limit_bytes=4 * 1024 * 1024
        ),
    )(own_rows)


def window_kernel(
    n_cycle, n_group, inner, halves, lanes, joined, step_rows,
    own_hbm, columns_ref, others_ref, int_ref, energy_ref, start_ref, vir_row_ref, aux_out, lag_out,
    own_ref, dens_ref, blocks_ref, stage, vir_col_ref, load_sem, dens_recv, dens_f32, pair_send, pair_recv, aux_sum, plane_send, plane_recv, plane_sum,
    line_send, line_recv, int_vmem, lag_acc, lag_send, lag_recv,
    int_sem, dens_ss, dens_rs, pair_ss, pair_rs, plane_ss, plane_rs, line_ss, line_rs,
    lag_ss, lag_rs,
):
    cyc = lax.axis_index("occ")
    grp = lax.axis_index("grp")
    n_dev = n_cycle * n_group
    me = cyc * n_group + grp
    outer = n_cycle // inner
    seat = lax.rem(cyc, inner)
    plane = cyc // inner
    tall_block = blocks_ref.shape[2]
    half_rows = lanes * tall_block
    rows = halves * half_rows
    depth = step_rows * lanes * 128
    n_steps = halves * tall_block // step_rows

    def int_copy(k):
        part = pl.ds(pl.multiple_of(k * depth, depth), depth)
        return pltpu.make_async_copy(int_ref.at[part], int_vmem.at[part], int_sem.at[k])

    own_load = pltpu.make_async_copy(own_hbm, own_ref, load_sem)
    own_load.start()
    barrier = pltpu.get_barrier_semaphore()

    @pl.loop(1, n_dev)
    def _(s):
        d = lax.rem(me + s, n_dev)
        pl.semaphore_signal(
            barrier, inc=1, device_id=(d // n_group, lax.rem(d, n_group)), device_id_type=MESH
        )

    @pl.loop(0, n_steps)
    def _(k):
        int_copy(k).start()

    def dens_copy(h, s):
        d = lax.rem(me + s, n_dev)
        part = pl.ds(h * lanes, lanes)
        return pltpu.make_async_remote_copy(
            src_ref=blocks_ref.at[d, part], dst_ref=dens_recv.at[s - 1, part],
            send_sem=dens_ss.at[h, s - 1], recv_sem=dens_rs.at[h, s - 1],
            device_id=(d // n_group, lax.rem(d, n_group)), device_id_type=MESH,
        )

    def pair_copy(s):
        return pltpu.make_async_remote_copy(
            src_ref=pair_send.at[s - 1], dst_ref=pair_recv.at[s - 1],
            send_sem=pair_ss.at[s - 1], recv_sem=pair_rs.at[s - 1],
            device_id=(cyc, lax.rem(grp + s, n_group)), device_id_type=MESH,
        )

    def plane_copy(s):
        q = lax.rem(seat + s, inner)
        return pltpu.make_async_remote_copy(
            src_ref=plane_send.at[s - 1], dst_ref=plane_recv.at[s - 1],
            send_sem=plane_ss.at[s - 1], recv_sem=plane_rs.at[s - 1],
            device_id=(plane * inner + q, grp), device_id_type=MESH,
        )

    def line_copy(s):
        z = lax.rem(plane + s, outer)
        return pltpu.make_async_remote_copy(
            src_ref=line_send.at[s - 1], dst_ref=line_recv.at[s - 1],
            send_sem=line_ss.at[s - 1], recv_sem=line_rs.at[s - 1],
            device_id=(z * inner + seat, grp), device_id_type=MESH,
        )

    def lag_copy(s):
        d = lax.rem(me + s, n_dev)
        return pltpu.make_async_remote_copy(
            src_ref=lag_send.at[d], dst_ref=lag_recv.at[s - 1],
            send_sem=lag_ss.at[s - 1], recv_sem=lag_rs.at[s - 1],
            device_id=(d // n_group, lax.rem(d, n_group)), device_id_type=MESH,
        )

    n_vir, n_aux = own_ref.shape
    vir_local, aux_local = n_vir // n_group, n_aux // n_cycle
    tall = joined * tall_block
    place, group = work_of(cyc, grp, n_cycle, n_group)
    shift = lax.rem(start_ref[0], n_cycle)
    by, side = 0, -1
    for s, (turned, on) in enumerate(route_plan(n_cycle)):
        by = jnp.where(shift == s, turned, by)
        side = jnp.where(shift == s, on, side)
    own_energy = energy_ref[lax.rem(place + by, n_cycle) * n_group + group]
    across = (((1,), (1,)), ((), ()))
    vir_col_ref[...] = jnp.broadcast_to(vir_row_ref[...], (128, n_vir)).T

    def densities(h):
        at = [pl.ds(g * vir_local + h * tall, tall) for g in range(n_group)]
        mine = jnp.concatenate([own_ref[rows, :] for rows in at], axis=0)
        theirs = jnp.concatenate(
            [
                others_ref[pl.ds(t * n_vir + rows.start, tall), :]
                for t in range(SHIFTS) for rows in at
            ],
            axis=0,
        )
        straight = lax.dot_general(
            mine, others_ref[...], across, preferred_element_type=jnp.float32
        )
        crossed = lax.dot_general(
            theirs, own_ref[...], across, preferred_element_type=jnp.float32
        )
        levels = jnp.concatenate([vir_col_ref[rows, 0:1] for rows in at], axis=0) + vir_row_ref[...]
        deep = n_group * tall
        combined = []
        for t in range(SHIFTS):
            partner = lax.rem(place + side * t + n_cycle, n_cycle)
            energy = own_energy + energy_ref[partner * n_group + group]
            pair = 2.0 * straight[:, t * n_vir:(t + 1) * n_vir] - crossed[t * deep:(t + 1) * deep]
            combined.append((pair / (energy - levels)).astype(jnp.bfloat16))
        value = jnp.dot(
            jnp.concatenate(combined, axis=1), others_ref[...], preferred_element_type=jnp.float32
        )
        for b in range(n_aux // 128):
            stage[pl.ds(b * deep, deep), :] = value[:, b * 128:(b + 1) * 128]
        for g in range(n_group):
            dens_ref[at[g], :] = value[g * tall:(g + 1) * tall].astype(dens_ref.dtype)

        @pl.loop(0, n_group)
        def _(g):
            picked = [
                jnp.concatenate(
                    [
                        stage[pl.ds(b * deep + g * tall + j, tall_block, stride=joined), :]
                        for b in range(n_aux // 128)
                    ],
                    axis=1,
                )
                for j in range(joined)
            ]
            for o in range(n_cycle):
                wide = jnp.concatenate(
                    [piece[:, o * aux_local:(o + 1) * aux_local] for piece in picked], axis=1
                ).astype(blocks_ref.dtype)
                for c in range(lanes):
                    blocks_ref[o * n_group + g, h * lanes + c] = wide[:, c * 128:(c + 1) * 128]

    own_load.wait()
    for h in range(halves):
        densities(h)
        if h == 0:
            pl.semaphore_wait(barrier, n_dev - 1)

        @pl.loop(1, n_dev)
        def _(s):
            dens_copy(h, s).start()

    def own_part(g):
        if columns_ref is not None:
            return columns_ref[g]
        width = aux_out.shape[1]
        return own_ref[:, pl.ds(pl.multiple_of(g * width, 128), width)]

    def aux_columns(g):
        return lax.dot_general(
            dens_ref[...], own_part(g), (((0,), (0,)), ((), ())),
            preferred_element_type=jnp.float32,
        ).reshape(aux_sum.shape)

    for s in range(1, n_group):
        pair_send[s - 1] = aux_columns(lax.rem(grp + s, n_group))
        pair_copy(s).start()
    aux_sum[...] = aux_columns(grp)
    for s in range(1, n_group):
        pair_copy(s).wait_recv()

        @pl.loop(0, n_cycle)
        def _(o):
            aux_sum[o] += pair_recv[s - 1, o]

    for s in range(1, inner):
        q = lax.rem(seat + s, inner)

        @pl.loop(0, outer)
        def _(z):
            plane_send[s - 1, z] = aux_sum[z * inner + q].astype(plane_send.dtype)

        plane_copy(s).start()

    def take_half(h):
        part = pl.ds(h * lanes, lanes)
        own_at = pl.ds(me * rows + h * half_rows, half_rows)
        dens_f32[own_at, :] = blocks_ref[me, part].astype(jnp.float32).reshape(half_rows, 128)

        @pl.loop(1, n_dev)
        def _(s):
            dens_copy(h, s).wait_recv()
            source = lax.rem(me - s + n_dev, n_dev)
            at = pl.ds(source * rows + h * half_rows, half_rows)
            block = dens_recv[s - 1, part].astype(jnp.float32)
            dens_f32[at, :] = block.reshape(half_rows, 128)

        steps = n_steps // halves

        @pl.loop(h * steps, (h + 1) * steps)
        def _(k):
            int_copy(k).wait()
            pieces = [
                dens_f32[
                    pl.ds(
                        h * half_rows + c * tall_block + (k - h * steps) * step_rows + j,
                        n_dev, stride=rows,
                    ), :
                ]
                for j in range(step_rows) for c in range(lanes)
            ]
            left = jnp.concatenate(pieces, axis=1).astype(jnp.bfloat16)
            at = pl.ds(pl.multiple_of(k * depth, depth), depth)
            lag_acc[...] += jnp.dot(left, int_vmem[at, :], preferred_element_type=jnp.float32)

    lag_acc[...] = jnp.zeros_like(lag_acc)
    for h in range(halves - 1):
        take_half(h)

    for s in range(1, inner):
        plane_copy(s).wait_recv()

    @pl.loop(0, outer)
    def _(z):
        block = aux_sum[z * inner + seat]
        for s in range(1, inner):
            block = block + plane_recv[s - 1, z].astype(jnp.float32)
        plane_sum[z] = block

    for s in range(1, outer):
        line_send[s - 1] = plane_sum[lax.rem(plane + s, outer)].astype(line_send.dtype)
        line_copy(s).start()

    take_half(halves - 1)

    device = lax.broadcasted_iota(jnp.int32, (n_dev, n_dev), 1)
    places, groups = work_of(device // n_group, device % n_group, n_cycle, n_group)
    places = places + by
    places = jnp.where(places >= n_cycle, places - n_cycle, places)
    orbital = lax.broadcasted_iota(jnp.int32, (n_dev, n_dev), 0)
    chosen = jnp.where(orbital == places * n_group + groups, 1.0, 0.0)
    lag_acc[...] = jnp.dot(
        chosen, lag_acc[...], preferred_element_type=jnp.float32, precision=lax.Precision.HIGHEST
    )

    orb_block = lag_out.shape[1]
    for o in range(n_cycle):
        for g in range(n_group):
            lag_send[o * n_group + g] = lag_acc[
                o * n_group:(o + 1) * n_group, g * orb_block:(g + 1) * orb_block
            ]

    @pl.loop(1, n_dev)
    def _(s):
        lag_copy(s).start()

    aux_total = plane_sum[plane]
    for s in range(1, outer):
        line_copy(s).wait_recv()
        aux_total = aux_total + line_recv[s - 1].astype(jnp.float32)
    aux_out[...] = aux_total

    lag_out[...] = lag_send[me]

    @pl.loop(1, n_dev)
    def _(s):
        lag_copy(s).wait_recv()
        lag_out[...] += lag_recv[s - 1]

    for s in range(1, n_group):
        pair_copy(s).wait_send()
    for s in range(1, inner):
        plane_copy(s).wait_send()
    for s in range(1, outer):
        line_copy(s).wait_send()

    @pl.loop(1, n_dev)
    def _(s):
        for h in range(halves):
            dens_copy(h, s).wait_send()
        lag_copy(s).wait_send()


def window(n_cycle, n_group, work_rows, others, int_rows, occ_energy, vir_energy, window_start):
    n_dev = n_cycle * n_group
    n_vir, n_aux = work_rows.shape
    row_block = n_aux // n_cycle
    col_block = n_aux // n_group
    depth, n_orb = int_rows.shape
    orb_block = n_orb // n_group
    _, _, joined, lanes, halves, tall_block = block_plan(n_vir, n_aux, n_cycle, n_group)
    blocks = (halves * lanes, tall_block, 128)
    step_rows = 2 if tall_block % 2 == 0 else 1
    rows = halves * lanes * tall_block
    inner = 4 if n_cycle % 4 == 0 else 1
    outer = n_cycle // inner
    tile = (row_block, col_block)
    anywhere = pl.BlockSpec(memory_space=pl.ANY)
    vmem = pl.BlockSpec(memory_space=pltpu.VMEM)
    smem = pl.BlockSpec(memory_space=pltpu.SMEM)
    dma = pltpu.SemaphoreType.DMA
    columns = None
    if col_block % 128:
        columns = work_rows.reshape(n_vir, n_group, col_block).transpose(1, 0, 2)
    body = functools.partial(
        window_kernel, n_cycle, n_group, inner, halves, lanes, joined, step_rows
    )

    def kernel(own_hbm, *refs):
        if columns is None:
            body(own_hbm, None, *refs)
        else:
            body(own_hbm, *refs)

    return pl.pallas_call(
        kernel,
        out_shape=(
            jax.ShapeDtypeStruct(tile, jnp.float32),
            jax.ShapeDtypeStruct((n_group, orb_block), jnp.float32),
        ),
        in_specs=[anywhere] + [vmem] * (columns is not None) + [vmem, anywhere, smem, smem, vmem],
        out_specs=(vmem, vmem),
        scratch_shapes=[
            pltpu.VMEM((n_vir, n_aux), jnp.bfloat16),
            pltpu.VMEM((n_vir, n_aux), jnp.bfloat16),
            pltpu.VMEM((n_dev,) + blocks, jnp.bfloat16),
            pltpu.VMEM((n_aux // 128 * n_group * joined * tall_block, 128), jnp.float32),
            pltpu.VMEM((n_vir, 128), jnp.float32),
            dma,
            pltpu.VMEM((n_dev - 1,) + blocks, jnp.bfloat16),
            pltpu.VMEM((n_dev * rows, 128), jnp.float32),
            pltpu.VMEM((n_group - 1, n_cycle) + tile, jnp.float32),
            pltpu.VMEM((n_group - 1, n_cycle) + tile, jnp.float32),
            pltpu.VMEM((n_cycle,) + tile, jnp.float32),
            pltpu.VMEM((inner - 1, outer) + tile, jnp.bfloat16),
            pltpu.VMEM((inner - 1, outer) + tile, jnp.bfloat16),
            pltpu.VMEM((outer,) + tile, jnp.float32),
            pltpu.VMEM((outer - 1,) + tile, jnp.bfloat16),
            pltpu.VMEM((outer - 1,) + tile, jnp.bfloat16),
            pltpu.VMEM((depth, n_orb), jnp.bfloat16),
            pltpu.VMEM((n_dev, n_orb), jnp.float32),
            pltpu.VMEM((n_dev, n_group, orb_block), jnp.float32),
            pltpu.VMEM((n_dev - 1, n_group, orb_block), jnp.float32),
            dma((halves * tall_block // step_rows,)),
            dma((halves, n_dev - 1)), dma((halves, n_dev - 1)),
            dma((n_group - 1,)), dma((n_group - 1,)),
            dma((inner - 1,)), dma((inner - 1,)),
            dma((outer - 1,)), dma((outer - 1,)),
            dma((n_dev - 1,)), dma((n_dev - 1,)),
        ],
        compiler_params=pltpu.CompilerParams(
            collective_id=0, has_side_effects=True, vmem_limit_bytes=44 * 1024 * 1024
        ),
    )(
        work_rows, *([] if columns is None else [columns]), others, int_rows, occ_energy,
        window_start, vir_energy[None, :],
    )


def local(b_factors, occ_energy, vir_energy, integrals, window_start):
    n_cycle = lax.axis_size("occ")
    n_group = lax.axis_size("grp")
    offset = jnp.mod(window_start[0], n_cycle)
    own_rows = b_factors[0]

    work_rows, others = lax.switch(
        offset,
        [
            functools.partial(gather, n_cycle, n_group, shift, by, side)
            for shift, (by, side) in enumerate(route_plan(n_cycle))
        ],
        own_rows,
    )
    int_rows = integrals.reshape(-1, integrals.shape[2])
    return window(
        n_cycle, n_group, work_rows, others, int_rows, occ_energy, vir_energy, window_start
    )


def solution(mesh):
    placed = (P(("occ", "grp"), None, None), P(), P(), P("grp", "occ", None), P())
    return jax.shard_map(
        local,
        mesh=mesh,
        in_specs=placed,
        out_specs=(P("occ", "grp"), P("occ", "grp")),
        check_vma=False,
    )
```

```python
import functools
import math

import jax
import jax.numpy as jnp
from jax import lax
from jax.experimental import pallas as pl
from jax.experimental.pallas import tpu as pltpu
from jax.sharding import PartitionSpec as P

MESH = pl.DeviceIdType.MESH
SHIFTS = 3


def work_of(cyc, grp, n_cycle, n_group):
    return cyc - cyc % 2 + grp % 2, grp - grp % 2 + cyc % 2


def route_plan(n_cycle):
    def cost(by):
        planes, rest = divmod(min(by, n_cycle - by), 4)
        z = planes + (0, 0.5 if planes else 1, 0.5 if planes else 1, 1)[rest] + 0.5
        y = (1, 1.5, 2, 1.5)[rest]
        return max(z, y), z

    plan = []
    for s in range(n_cycle):
        later = (s + 2) % n_cycle
        plan.append((later, 1) if cost(later) < cost(s) else (s, -1))
    return plan


def block_plan(n_vir, n_aux, n_cycle, n_group):
    aux_local, vir_local = n_aux // n_cycle, n_vir // n_group
    joined = 128 // math.gcd(aux_local, 128)
    lanes = joined * aux_local // 128
    halves = 2 if vir_local % (32 * joined) == 0 else 1
    return aux_local, vir_local, joined, lanes, halves, vir_local // joined // halves


def ferried(n_cycle, chunks, by):
    planes, rest = divmod(min(by, n_cycle - by), 4)
    return max(1, chunks // (2 * planes + 2)) if planes and rest in (1, 2) else 0


def gather_kernel(
    n_cycle, n_group, chunks, by, side,
    own, work, blocks, hop, copy_sem, swap_ss, swap_rs, out_ss, hop_rs, fwd_ss, far_rs, near_ss, near_rs,
    turn_ss, turn_rs, ferry, ferry_ss, ferry_rs,
):
    cyc = lax.axis_index("occ")
    grp = lax.axis_index("grp")
    x, y, core = lax.rem(cyc, 2), lax.rem(cyc // 2, 2), lax.rem(grp, 2)
    n_vir = own.shape[0]
    size = n_vir // chunks
    half = chunks // 2
    here, near, far = (blocks.at[pl.ds(t * n_vir, n_vir)] for t in range(SHIFTS))
    diagonal = (cyc + 1 - 2 * x, grp + 1 - 2 * core)
    twin = (cyc, grp + 1 - 2 * core)
    y_mate = (cyc + 2 - 4 * y, grp)
    onward = (lax.rem(cyc + n_cycle - 4 * side, n_cycle), grp)
    back = (lax.rem(cyc + n_cycle + 4 * side, n_cycle), grp)
    first, lower = (y, core) if side < 0 else (1 - y, 1 - core)
    place, group = cyc - x + core, grp - core + x
    source = (lax.rem(place + by, n_cycle), group)
    n_ferry = ferried(n_cycle, chunks, by)

    def goal_of(cyc):
        goal = lax.rem(cyc + n_cycle - by, n_cycle)
        goal_x = lax.rem(goal, 2)
        return (goal - goal_x + core, grp - core + goal_x)

    def climbs(cyc):
        seat = lax.rem(cyc, 4)
        if 2 * by <= n_cycle:
            return (seat < by % 4).astype(jnp.int32)
        return (seat >= by % 4).astype(jnp.int32)

    goal = goal_of(cyc)
    load, carry = climbs(cyc), climbs(y_mate[0])
    source_y = lax.rem(source[0] // 2, 2)
    source_mate = (source[0] + 2 - 4 * source_y, group)
    barrier = pltpu.get_barrier_semaphore()
    for other in (twin, y_mate, back) + ((source,) if by else ()):
        pl.semaphore_signal(barrier, inc=1, device_id=other, device_id_type=MESH)

    @pl.when(x != core)
    def _():
        pl.semaphore_signal(barrier, inc=1, device_id=diagonal, device_id_type=MESH)

    if n_ferry:
        @pl.when(climbs(source[0]) == 1)
        def _():
            pl.semaphore_signal(barrier, inc=1, device_id=source_mate, device_id_type=MESH)

    peers = 3 + (by != 0) + lax.rem(x + core, 2)
    pl.semaphore_wait(barrier, peers + carry if n_ferry else peers)

    def part(c):
        return pl.ds(c * size, size)

    def remote(src, dst, send_sem, recv_sem, to):
        return pltpu.make_async_remote_copy(
            src_ref=src, dst_ref=dst, send_sem=send_sem, recv_sem=recv_sem,
            device_id=to, device_id_type=MESH,
        )

    def swap_copy(c):
        return remote(own.at[part(c)], here.at[part(c)], swap_ss.at[c], swap_rs.at[c], diagonal)

    def turn_copy(c):
        if by:
            return remote(own.at[part(c)], work.at[part(c)], turn_ss.at[c], turn_rs.at[c], goal)
        return pltpu.make_async_copy(here.at[part(c)], work.at[part(c)], turn_rs.at[c])

    def ferry_copy(c):
        return remote(own.at[part(c)], ferry.at[part(c)], turn_ss.at[c], ferry_rs.at[c], y_mate)

    def carry_copy(c):
        return remote(
            ferry.at[part(c)], work.at[part(c)], ferry_ss.at[c], turn_rs.at[c], goal_of(y_mate[0])
        )

    def near_copy(c, source):
        return remote(source.at[part(c)], near.at[part(c)], near_ss.at[c], near_rs.at[c], twin)

    def direct_copy(c, source):
        return remote(source.at[part(c)], far.at[part(c)], out_ss.at[c], far_rs.at[c], y_mate)

    def hop_copy(c, source):
        return remote(
            source.at[part(c)], hop.at[part(c % half)], out_ss.at[c], hop_rs.at[c % half],
            y_mate if c < half else onward,
        )

    def onward_copy(c):
        return remote(hop.at[part(c)], far.at[part(c)], fwd_ss.at[c], far_rs.at[c], onward)

    def across_copy(c):
        return remote(
            hop.at[part(c)], far.at[part(c + half)], fwd_ss.at[c], far_rs.at[c + half], y_mate
        )

    def pass_on(c, source):
        @pl.when(first == 0)
        def _():
            direct_copy(c, source).start()

        @pl.when(first == 1)
        def _():
            hop_copy(c, source).start()

        @pl.when(lower == 0)
        def _():
            near_copy(c, source).start()

    order = [c // 2 + half * (c % 2) for c in range(chunks)]
    turns = iter(range(chunks) if by else ())

    def turn(count):
        for c in [c for _, c in zip(range(count), turns)]:
            if c < n_ferry:
                @pl.when(load == 0)
                def _():
                    turn_copy(c).start()

                @pl.when(load == 1)
                def _():
                    ferry_copy(c).start()
            else:
                turn_copy(c).start()

    keep = pltpu.make_async_copy(own, here, copy_sem)

    turn(2)

    @pl.when(x == core)
    def _():
        for c in order:
            pass_on(c, own)
        keep.start()

    @pl.when(x != core)
    def _():
        for c in order:
            swap_copy(c).start()
        for c in order:
            swap_copy(c).wait_recv()
            pass_on(c, here)

    turn(2)
    for c in range(n_ferry):
        @pl.when(carry == 1)
        def _():
            ferry_copy(c).wait_recv()
            carry_copy(c).start()

    for c in range(half):
        hop_copy(c, own).wait_recv()

        @pl.when(first == 0)
        def _():
            onward_copy(c).start()

        @pl.when(first == 1)
        def _():
            across_copy(c).start()

        turn(1)

    turn(chunks)

    @pl.when(x == core)
    def _():
        keep.wait()

    if not by:
        for c in range(chunks):
            turn_copy(c).start()

    for c in order:
        direct_copy(c, own).wait_recv()

        @pl.when(lower == 1)
        def _():
            near_copy(c, far).start()

    for c in range(chunks):
        near_copy(c, far).wait_recv()
        near_copy(c, far).wait_send()
        direct_copy(c, own).wait_send()
        if by:
            turn_copy(c).wait_recv()
            turn_copy(c).wait_send()
        else:
            turn_copy(c).wait()
    for c in range(half):
        onward_copy(c).wait_send()

    for c in range(n_ferry):
        @pl.when(carry == 1)
        def _():
            carry_copy(c).wait_send()

    @pl.when(x != core)
    def _():
        for c in range(chunks):
            swap_copy(c).wait_send()


def gather(n_cycle, n_group, shift, by, side, own_rows):
    n_vir, n_aux = own_rows.shape
    chunks = 8
    dma = pltpu.SemaphoreType.DMA
    anywhere = pl.BlockSpec(memory_space=pl.ANY)
    return pl.pallas_call(
        functools.partial(gather_kernel, n_cycle, n_group, chunks, by, side),
        out_shape=(
            jax.ShapeDtypeStruct((n_vir, n_aux), own_rows.dtype),
            jax.ShapeDtypeStruct((SHIFTS * n_vir, n_aux), own_rows.dtype),
        ),
        in_specs=[anywhere],
        out_specs=(anywhere, anywhere),
        scratch_shapes=[
            pltpu.VMEM((n_vir // 2, n_aux), own_rows.dtype), dma,
            dma((chunks,)), dma((chunks,)), dma((chunks,)), dma((chunks // 2,)),
            dma((chunks // 2,)), dma((chunks,)), dma((chunks,)), dma((chunks,)),
            dma((chunks,)), dma((chunks,)),
            pltpu.VMEM((n_vir // 2, n_aux), own_rows.dtype), dma((chunks // 2,)), dma((chunks // 2,)),
        ],
        compiler_params=pltpu.CompilerParams(
            collective_id=1 + shift, has_side_effects=True, vmem_limit_bytes=4 * 1024 * 1024
        ),
    )(own_rows)


def window_kernel(
    n_cycle, n_group, inner, halves, lanes, joined, step_rows,
    own_hbm, columns_ref, others_ref, int_ref, energy_ref, start_ref, vir_row_ref, aux_out, lag_out,
    own_ref, dens_ref, blocks_ref, stage, vir_col_ref, load_sem, dens_recv, dens_f32, pair_send, pair_recv, aux_sum, plane_send, plane_recv, plane_sum,
    line_send, line_recv, int_vmem, lag_acc, lag_send, lag_recv,
    int_sem, dens_ss, dens_rs, pair_ss, pair_rs, plane_ss, plane_rs, line_ss, line_rs,
    lag_ss, lag_rs,
):
    cyc = lax.axis_index("occ")
    grp = lax.axis_index("grp")
    n_dev = n_cycle * n_group
    me = cyc * n_group + grp
    outer = n_cycle // inner
    seat = lax.rem(cyc, inner)
    plane = cyc // inner
    tall_block = blocks_ref.shape[2]
    half_rows = lanes * tall_block
    rows = halves * half_rows
    depth = step_rows * lanes * 128
    n_steps = halves * tall_block // step_rows

    def int_copy(k):
        part = pl.ds(pl.multiple_of(k * depth, depth), depth)
        return pltpu.make_async_copy(int_ref.at[part], int_vmem.at[part], int_sem.at[k])

    own_load = pltpu.make_async_copy(own_hbm, own_ref, load_sem)
    own_load.start()
    barrier = pltpu.get_barrier_semaphore()

    @pl.loop(1, n_dev)
    def _(s):
        d = lax.rem(me + s, n_dev)
        pl.semaphore_signal(
            barrier, inc=1, device_id=(d // n_group, lax.rem(d, n_group)), device_id_type=MESH
        )

    @pl.loop(0, n_steps)
    def _(k):
        int_copy(k).start()

    def dens_copy(h, s):
        d = lax.rem(me + s, n_dev)
        part = pl.ds(h * lanes, lanes)
        return pltpu.make_async_remote_copy(
            src_ref=blocks_ref.at[d, part], dst_ref=dens_recv.at[s - 1, part],
            send_sem=dens_ss.at[h, s - 1], recv_sem=dens_rs.at[h, s - 1],
            device_id=(d // n_group, lax.rem(d, n_group)), device_id_type=MESH,
        )

    def pair_copy(s):
        return pltpu.make_async_remote_copy(
            src_ref=pair_send.at[s - 1], dst_ref=pair_recv.at[s - 1],
            send_sem=pair_ss.at[s - 1], recv_sem=pair_rs.at[s - 1],
            device_id=(cyc, lax.rem(grp + s, n_group)), device_id_type=MESH,
        )

    def plane_copy(s):
        q = lax.rem(seat + s, inner)
        return pltpu.make_async_remote_copy(
            src_ref=plane_send.at[s - 1], dst_ref=plane_recv.at[s - 1],
            send_sem=plane_ss.at[s - 1], recv_sem=plane_rs.at[s - 1],
            device_id=(plane * inner + q, grp), device_id_type=MESH,
        )

    def line_copy(s):
        z = lax.rem(plane + s, outer)
        return pltpu.make_async_remote_copy(
            src_ref=line_send.at[s - 1], dst_ref=line_recv.at[s - 1],
            send_sem=line_ss.at[s - 1], recv_sem=line_rs.at[s - 1],
            device_id=(z * inner + seat, grp), device_id_type=MESH,
        )

    def lag_copy(s):
        d = lax.rem(me + s, n_dev)
        return pltpu.make_async_remote_copy(
            src_ref=lag_send.at[d], dst_ref=lag_recv.at[s - 1],
            send_sem=lag_ss.at[s - 1], recv_sem=lag_rs.at[s - 1],
            device_id=(d // n_group, lax.rem(d, n_group)), device_id_type=MESH,
        )

    n_vir, n_aux = own_ref.shape
    vir_local, aux_local = n_vir // n_group, n_aux // n_cycle
    tall = joined * tall_block
    place, group = work_of(cyc, grp, n_cycle, n_group)
    shift = lax.rem(start_ref[0], n_cycle)
    by, side = 0, -1
    for s, (turned, on) in enumerate(route_plan(n_cycle)):
        by = jnp.where(shift == s, turned, by)
        side = jnp.where(shift == s, on, side)
    own_energy = energy_ref[lax.rem(place + by, n_cycle) * n_group + group]
    across = (((1,), (1,)), ((), ()))
    vir_col_ref[...] = jnp.broadcast_to(vir_row_ref[...], (128, n_vir)).T

    def densities(h):
        at = [pl.ds(g * vir_local + h * tall, tall) for g in range(n_group)]
        mine = jnp.concatenate([own_ref[rows, :] for rows in at], axis=0)
        theirs = jnp.concatenate(
            [
                others_ref[pl.ds(t * n_vir + rows.start, tall), :]
                for t in range(SHIFTS) for rows in at
            ],
            axis=0,
        )
        straight = lax.dot_general(
            mine, others_ref[...], across, preferred_element_type=jnp.float32
        )
        crossed = lax.dot_general(
            theirs, own_ref[...], across, preferred_element_type=jnp.float32
        )
        levels = jnp.concatenate([vir_col_ref[rows, 0:1] for rows in at], axis=0) + vir_row_ref[...]
        deep = n_group * tall
        combined = []
        for t in range(SHIFTS):
            partner = lax.rem(place + side * t + n_cycle, n_cycle)
            energy = own_energy + energy_ref[partner * n_group + group]
            pair = 2.0 * straight[:, t * n_vir:(t + 1) * n_vir] - crossed[t * deep:(t + 1) * deep]
            combined.append((pair / (energy - levels)).astype(jnp.bfloat16))
        value = jnp.dot(
            jnp.concatenate(combined, axis=1), others_ref[...], preferred_element_type=jnp.float32
        )
        for b in range(n_aux // 128):
            stage[pl.ds(b * deep, deep), :] = value[:, b * 128:(b + 1) * 128]
        for g in range(n_group):
            dens_ref[at[g], :] = value[g * tall:(g + 1) * tall].astype(dens_ref.dtype)

        @pl.loop(0, n_group)
        def _(g):
            picked = [
                jnp.concatenate(
                    [
                        stage[pl.ds(b * deep + g * tall + j, tall_block, stride=joined), :]
                        for b in range(n_aux // 128)
                    ],
                    axis=1,
                )
                for j in range(joined)
            ]
            for o in range(n_cycle):
                wide = jnp.concatenate(
                    [piece[:, o * aux_local:(o + 1) * aux_local] for piece in picked], axis=1
                ).astype(blocks_ref.dtype)
                for c in range(lanes):
                    blocks_ref[o * n_group + g, h * lanes + c] = wide[:, c * 128:(c + 1) * 128]

    own_load.wait()
    for h in range(halves):
        densities(h)
        if h == 0:
            pl.semaphore_wait(barrier, n_dev - 1)

        @pl.loop(1, n_dev, unroll=n_dev <= 64)
        def _(s):
            dens_copy(h, s).start()

    def own_part(g):
        if columns_ref is not None:
            return columns_ref[g]
        width = aux_out.shape[1]
        return own_ref[:, pl.ds(pl.multiple_of(g * width, 128), width)]

    def aux_columns(g):
        return lax.dot_general(
            dens_ref[...], own_part(g), (((0,), (0,)), ((), ())),
            preferred_element_type=jnp.float32,
        ).reshape(aux_sum.shape)

    for s in range(1, n_group):
        pair_send[s - 1] = aux_columns(lax.rem(grp + s, n_group))
        pair_copy(s).start()
    aux_sum[...] = aux_columns(grp)
    for s in range(1, n_group):
        pair_copy(s).wait_recv()

        @pl.loop(0, n_cycle)
        def _(o):
            aux_sum[o] += pair_recv[s - 1, o]

    for s in range(1, inner):
        q = lax.rem(seat + s, inner)

        @pl.loop(0, outer)
        def _(z):
            plane_send[s - 1, z] = aux_sum[z * inner + q].astype(plane_send.dtype)

        plane_copy(s).start()

    def take_half(h):
        part = pl.ds(h * lanes, lanes)
        own_at = pl.ds(me * rows + h * half_rows, half_rows)
        dens_f32[own_at, :] = blocks_ref[me, part].astype(jnp.float32).reshape(half_rows, 128)

        @pl.loop(1, n_dev, unroll=n_dev <= 64)
        def _(s):
            dens_copy(h, s).wait_recv()
            source = lax.rem(me - s + n_dev, n_dev)
            at = pl.ds(source * rows + h * half_rows, half_rows)
            block = dens_recv[s - 1, part].astype(jnp.float32)
            dens_f32[at, :] = block.reshape(half_rows, 128)

        steps = n_steps // halves

        @pl.loop(h * steps, (h + 1) * steps)
        def _(k):
            int_copy(k).wait()
            pieces = [
                dens_f32[
                    pl.ds(
                        h * half_rows + c * tall_block + (k - h * steps) * step_rows + j,
                        n_dev, stride=rows,
                    ), :
                ]
                for j in range(step_rows) for c in range(lanes)
            ]
            left = jnp.concatenate(pieces, axis=1).astype(jnp.bfloat16)
            at = pl.ds(pl.multiple_of(k * depth, depth), depth)
            lag_acc[...] += jnp.dot(left, int_vmem[at, :], preferred_element_type=jnp.float32)

    lag_acc[...] = jnp.zeros_like(lag_acc)
    for h in range(halves - 1):
        take_half(h)

    for s in range(1, inner):
        plane_copy(s).wait_recv()

    @pl.loop(0, outer)
    def _(z):
        block = aux_sum[z * inner + seat]
        for s in range(1, inner):
            block = block + plane_recv[s - 1, z].astype(jnp.float32)
        plane_sum[z] = block

    for s in range(1, outer):
        line_send[s - 1] = plane_sum[lax.rem(plane + s, outer)].astype(line_send.dtype)
        line_copy(s).start()

    take_half(halves - 1)

    device = lax.broadcasted_iota(jnp.int32, (n_dev, n_dev), 1)
    places, groups = work_of(device // n_group, device % n_group, n_cycle, n_group)
    places = places + by
    places = jnp.where(places >= n_cycle, places - n_cycle, places)
    orbital = lax.broadcasted_iota(jnp.int32, (n_dev, n_dev), 0)
    chosen = jnp.where(orbital == places * n_group + groups, 1.0, 0.0)
    lag_acc[...] = jnp.dot(
        chosen, lag_acc[...], preferred_element_type=jnp.float32, precision=lax.Precision.HIGHEST
    )

    orb_block = lag_out.shape[1]
    for o in range(n_cycle):
        for g in range(n_group):
            lag_send[o * n_group + g] = lag_acc[
                o * n_group:(o + 1) * n_group, g * orb_block:(g + 1) * orb_block
            ]

    @pl.loop(1, n_dev, unroll=n_dev <= 64)
    def _(s):
        lag_copy(s).start()

    aux_total = plane_sum[plane]
    for s in range(1, outer):
        line_copy(s).wait_recv()
        aux_total = aux_total + line_recv[s - 1].astype(jnp.float32)
    aux_out[...] = aux_total

    @pl.loop(1, n_dev)
    def _(s):
        lag_copy(s).wait_recv()

    lag_out[...] = lag_send[me] + jnp.sum(lag_recv[...], axis=0)

    for s in range(1, n_group):
        pair_copy(s).wait_send()
    for s in range(1, inner):
        plane_copy(s).wait_send()
    for s in range(1, outer):
        line_copy(s).wait_send()

    @pl.loop(1, n_dev)
    def _(s):
        for h in range(halves):
            dens_copy(h, s).wait_send()
        lag_copy(s).wait_send()


def window(n_cycle, n_group, work_rows, others, int_rows, occ_energy, vir_energy, window_start):
    n_dev = n_cycle * n_group
    n_vir, n_aux = work_rows.shape
    row_block = n_aux // n_cycle
    col_block = n_aux // n_group
    depth, n_orb = int_rows.shape
    orb_block = n_orb // n_group
    _, _, joined, lanes, halves, tall_block = block_plan(n_vir, n_aux, n_cycle, n_group)
    blocks = (halves * lanes, tall_block, 128)
    step_rows = 2 if tall_block % 2 == 0 else 1
    rows = halves * lanes * tall_block
    inner = 4 if n_cycle % 4 == 0 else 1
    outer = n_cycle // inner
    tile = (row_block, col_block)
    anywhere = pl.BlockSpec(memory_space=pl.ANY)
    vmem = pl.BlockSpec(memory_space=pltpu.VMEM)
    smem = pl.BlockSpec(memory_space=pltpu.SMEM)
    dma = pltpu.SemaphoreType.DMA
    columns = None
    if col_block % 128:
        columns = work_rows.reshape(n_vir, n_group, col_block).transpose(1, 0, 2)
    body = functools.partial(
        window_kernel, n_cycle, n_group, inner, halves, lanes, joined, step_rows
    )

    def kernel(own_hbm, *refs):
        if columns is None:
            body(own_hbm, None, *refs)
        else:
            body(own_hbm, *refs)

    return pl.pallas_call(
        kernel,
        out_shape=(
            jax.ShapeDtypeStruct(tile, jnp.float32),
            jax.ShapeDtypeStruct((n_group, orb_block), jnp.float32),
        ),
        in_specs=[anywhere] + [vmem] * (columns is not None) + [vmem, anywhere, smem, smem, vmem],
        out_specs=(vmem, vmem),
        scratch_shapes=[
            pltpu.VMEM((n_vir, n_aux), jnp.bfloat16),
            pltpu.VMEM((n_vir, n_aux), jnp.bfloat16),
            pltpu.VMEM((n_dev,) + blocks, jnp.bfloat16),
            pltpu.VMEM((n_aux // 128 * n_group * joined * tall_block, 128), jnp.float32),
            pltpu.VMEM((n_vir, 128), jnp.float32),
            dma,
            pltpu.VMEM((n_dev - 1,) + blocks, jnp.bfloat16),
            pltpu.VMEM((n_dev * rows, 128), jnp.float32),
            pltpu.VMEM((n_group - 1, n_cycle) + tile, jnp.float32),
            pltpu.VMEM((n_group - 1, n_cycle) + tile, jnp.float32),
            pltpu.VMEM((n_cycle,) + tile, jnp.float32),
            pltpu.VMEM((inner - 1, outer) + tile, jnp.bfloat16),
            pltpu.VMEM((inner - 1, outer) + tile, jnp.bfloat16),
            pltpu.VMEM((outer,) + tile, jnp.float32),
            pltpu.VMEM((outer - 1,) + tile, jnp.bfloat16),
            pltpu.VMEM((outer - 1,) + tile, jnp.bfloat16),
            pltpu.VMEM((depth, n_orb), jnp.bfloat16),
            pltpu.VMEM((n_dev, n_orb), jnp.float32),
            pltpu.VMEM((n_dev, n_group, orb_block), jnp.float32),
            pltpu.VMEM((n_dev - 1, n_group, orb_block), jnp.float32),
            dma((halves * tall_block // step_rows,)),
            dma((halves, n_dev - 1)), dma((halves, n_dev - 1)),
            dma((n_group - 1,)), dma((n_group - 1,)),
            dma((inner - 1,)), dma((inner - 1,)),
            dma((outer - 1,)), dma((outer - 1,)),
            dma((n_dev - 1,)), dma((n_dev - 1,)),
        ],
        compiler_params=pltpu.CompilerParams(
            collective_id=0, has_side_effects=True, vmem_limit_bytes=44 * 1024 * 1024
        ),
    )(
        work_rows, *([] if columns is None else [columns]), others, int_rows, occ_energy,
        window_start, vir_energy[None, :],
    )


def local(b_factors, occ_energy, vir_energy, integrals, window_start):
    n_cycle = lax.axis_size("occ")
    n_group = lax.axis_size("grp")
    offset = jnp.mod(window_start[0], n_cycle)
    own_rows = b_factors[0]

    work_rows, others = lax.switch(
        offset,
        [
            functools.partial(gather, n_cycle, n_group, shift, by, side)
            for shift, (by, side) in enumerate(route_plan(n_cycle))
        ],
        own_rows,
    )
    int_rows = integrals.reshape(-1, integrals.shape[2])
    return window(
        n_cycle, n_group, work_rows, others, int_rows, occ_energy, vir_energy, window_start
    )


def solution(mesh):
    placed = (P(("occ", "grp"), None, None), P(), P(), P("grp", "occ", None), P())
    return jax.shard_map(
        local,
        mesh=mesh,
        in_specs=placed,
        out_specs=(P("occ", "grp"), P("occ", "grp")),
        check_vma=False,
    )
```
